256 devices in a mesh: wide: 8 (over y, core), narrow: 4 (over z_lo), net: 8 (over z_hi, x).
Axes of the slice: x: 4, y: 4, z: 8 (z_hi: 2, z_lo: 4; z = z_hi * 4 + z_lo), core: 2. Of those that a mesh axis runs over, the one named last changes fastest.
Arguments:
- fields: float32 [4, 64, 32, 1024], P(None, 'net', 'wide', 'narrow'), may hold values from -7.5 to 7.5
- conv1_weight: bfloat16 [27, 32, 4], replicated, may hold values from -0.625 to 0.625
- conv1_bias: float32 [32], replicated, may hold values from -6 to 6
- conv2_weight: bfloat16 [27, 6, 32], replicated, may hold values from -0.21875 to 0.21875
Outputs:
- advanced: float32 [4, 64, 32, 1024], P(None, 'net', 'wide', 'narrow')
The draws below stay inside these ranges and needn't reach their ends.
All inputs are finite; a program needn't handle non-finite values.
Results may differ from the reference program's by a relative error of at most 0.0028.
Values may be sent and summed in bfloat16 or wider, within the bound.
No kernel may reach another device: no remote copies, remote signals or barrier semaphores. Data moves between devices by JAX's collectives and lax.ppermute only.
A program may use at most 64 MiB of HBM per device.

```python
import jax
import jax.numpy as jnp
from jax import lax

FIELDS = 4
STRESS = 6
HIDDEN_SIZE = 32
NX = 32
NY = 1024
NZ = 64


def level_of(key, extent, cuts, low, largest):
    level, own = 1.0, jax.random.fold_in(key, 6)
    for axis_at, shards_of in cuts:
        draws = jnp.exp(jax.random.uniform(jax.random.fold_in(own, axis_at), (shards_of,), jnp.float32, low / len(cuts), largest / len(cuts)))
        level = level * jnp.repeat(draws, extent[axis_at] // shards_of).reshape([-1 if axis == axis_at else 1 for axis in range(len(extent))])
    return level


def bell_draw(own_key, dims, scale, reach, shards=(), kind=jnp.bfloat16):
    factor_of = level_of(own_key, dims, shards, -0.22, 0.18) if shards else 1.0
    values = jax.random.normal(own_key, dims, jnp.float32) * scale * factor_of
    return jnp.minimum(jnp.maximum(values, -reach), reach).astype(kind)


def setup_inputs(seed: int = 0) -> dict:
    seeds = jax.random.split(jax.random.key(seed), 5)
    fields = bell_draw(seeds[0], (FIELDS, NZ, NX, NY), 3.0, 7.5, ((1, 8), (2, 8), (3, 4)), jnp.float32)
    conv1_weight = jnp.clip(jax.random.uniform(seeds[1], (27, HIDDEN_SIZE, FIELDS), jnp.float32, -0.625, 0.625), -0.625, 0.625).astype(jnp.bfloat16)
    conv1_bias = bell_draw(seeds[2], (HIDDEN_SIZE,), 2.0, 6.0, (), jnp.float32)
    conv2_weight = jnp.clip(jax.random.uniform(seeds[3], (27, STRESS, HIDDEN_SIZE), jnp.float32, -0.21875, 0.21875), -0.21875, 0.21875).astype(jnp.bfloat16)
    return {"fields": fields, "conv1_weight": conv1_weight, "conv1_bias": conv1_bias, "conv2_weight": conv2_weight}


time_step = 0.2
viscosity = 0.05


def neighbour(field, offset, axis):
    return jnp.roll(field, -offset, axis=axis)


def coarsen(fields):
    channels, deep_cells, row_cells, col_cells = fields.shape
    grouped = fields.reshape(channels, deep_cells // 2, 2, row_cells // 2, 2, col_cells // 2, 2)
    return jnp.mean(grouped, axis=(2, 4, 6))


def convolve(inputs, weights):
    padded = jnp.pad(inputs.astype(jnp.float32), ((0, 0), (1, 1), (1, 1), (1, 1)), mode="wrap")
    outputs = weights.shape[1]
    channels = weights.shape[2]
    kernel = weights.astype(jnp.float32).reshape(3, 3, 3, outputs, channels).transpose(3, 4, 0, 1, 2)
    result = lax.conv_general_dilated(padded[None], kernel, (1, 1, 1), "VALID", dimension_numbers=("NCDHW", "OIDHW", "NCDHW"), precision=lax.Precision.HIGHEST, preferred_element_type=jnp.float32)
    return result[0]


def derivative(field, axis):
    return (neighbour(field, 1, axis) - neighbour(field, -1, axis)) * 0.25


def divergence(stress):
    values = stress.astype(jnp.float32)
    force_x = derivative(values[0], 1) + derivative(values[3], 2) + derivative(values[4], 0)
    force_y = derivative(values[3], 1) + derivative(values[1], 2) + derivative(values[5], 0)
    force_z = derivative(values[4], 1) + derivative(values[5], 2) + derivative(values[2], 0)
    return jnp.stack([force_x, force_y, force_z])


def upsample(field):
    return jnp.repeat(jnp.repeat(jnp.repeat(field, 2, 0), 2, 1), 2, 2)


def tendency(state, forcing):
    results = []
    for index in range(state.shape[0]):
        field = state[index]
        grad_z = (neighbour(field, 1, 0) - neighbour(field, -1, 0)) * 0.5
        grad_x = (neighbour(field, 1, 1) - neighbour(field, -1, 1)) * 0.5
        grad_y = (neighbour(field, 1, 2) - neighbour(field, -1, 2)) * 0.5
        spread = neighbour(field, 1, 0) + neighbour(field, -1, 0) + neighbour(field, 1, 1) + neighbour(field, -1, 1) + neighbour(field, 1, 2) + neighbour(field, -1, 2) - 6.0 * field
        change = viscosity * spread - (state[0] * grad_x + state[1] * grad_y + state[2] * grad_z)
        if index < 3:
            change = change + upsample(forcing[index])
        results.append(change)
    return jnp.stack(results)


def reference(fields, conv1_weight, conv1_bias, conv2_weight):
    def rate(state):
        coarse = lax.optimization_barrier(coarsen(state).astype(jnp.bfloat16))
        hidden = jax.nn.gelu(convolve(coarse, conv1_weight) + conv1_bias[:, None, None, None], approximate=True)
        hidden = lax.optimization_barrier(hidden.astype(jnp.bfloat16))
        stress = lax.optimization_barrier(convolve(hidden, conv2_weight).astype(jnp.bfloat16))
        return tendency(state, divergence(stress))

    section_one = fields + time_step * rate(fields)
    section_two = 0.75 * fields + 0.25 * (section_one + time_step * rate(section_one))
    return fields / 3.0 + (2.0 / 3.0) * (section_two + time_step * rate(section_two))
```

```python
import functools

import jax
import jax.numpy as jnp
import numpy as np
from jax import lax
from jax.experimental import pallas as pl
from jax.experimental.pallas import tpu as pltpu
from jax.sharding import PartitionSpec as P

time_step = 0.2
viscosity = 0.05
EDGE = 9
HALF = 64
F32 = jnp.float32
BF16 = jnp.bfloat16
HIGH = lax.Precision.HIGHEST
VM = pl.BlockSpec(memory_space=pltpu.VMEM)
SM = pl.BlockSpec(memory_space=pltpu.SMEM)


def split_parity():
    m = np.zeros((256, 256), np.float32)
    for l in range(128):
        m[2 * l, l] = 1.0
        m[2 * l + 1, 128 + l] = 1.0
    return m


def row_order():
    m = np.zeros((256, 256), np.float32)
    for z in range(8):
        for x in range(4):
            for p in range(2):
                for c in range(4):
                    m[((z * 4 + x) * 2 + p) * 4 + c, ((p * 4 + c) * 8 + z) * 4 + x] = 1.0
    return m


def place_conv1():
    m = np.zeros((27, 4, 8, 512), np.float32)
    for dz in range(3):
        for dx in range(3):
            for dy in range(3):
                for c in range(4):
                    for xo in range(8):
                        xi = xo + 1 + dx
                        m[9 * dz + 3 * dx + dy, c, xo, ((dz * 3 + dy) * 12 + xi) * 4 + c] = 1.0
    return m.reshape(108, 4096)


def place_conv2():
    m = np.zeros((3, 32, 6, 8, 32), np.float32)
    for dx in range(3):
        for h in range(32):
            for xo in range(6):
                m[dx, h, xo, xo + dx, h] = 1.0
    return m.reshape(96, 6 * 256)


def divergence_matrix():
    m = np.zeros((4, 2, 4, 5, 6, 8), np.float32)
    sx, sy, sz = (0, 3, 4), (3, 1, 5), (4, 5, 2)
    for x in range(4):
        for comp in range(3):
            m[x, :, comp, 1, x + 2, sx[comp]] += 0.25
            m[x, :, comp, 1, x, sx[comp]] -= 0.25
            m[x, :, comp, 4, x + 1, sy[comp]] += 0.25
            m[x, :, comp, 3, x + 1, sy[comp]] -= 0.25
            m[x, :, comp, 2, x + 1, sz[comp]] += 0.25
            m[x, :, comp, 0, x + 1, sz[comp]] -= 0.25
    return m.reshape(32, 240)


def call(kernel, outs, scratch, *args):
    specs = [SM if a.ndim == 1 else VM for a in args]
    return pl.pallas_call(
        kernel,
        out_shape=[jax.ShapeDtypeStruct(s, d) for s, d in outs],
        in_specs=specs,
        out_specs=[VM] * len(outs),
        scratch_shapes=scratch,
    )(*args)


def exact(a, b, dims=(((1,), (0,)), ((), ()))):
    return lax.dot_general(a, b, dims, precision=HIGH, preferred_element_type=F32)


def lanes_of(shape):
    return lax.broadcasted_iota(jnp.int32, shape, len(shape) - 1)


def pack_kernel(core_ref, fields_ref, parity_ref, order_ref, native_ref, same_ref, cross_ref, flat):
    core = core_ref[0]
    for c in range(4):
        for z in range(8):
            flat[pl.ds((c * 8 + z) * 4, 4), :] = fields_ref[c, z]
    parts = exact(flat[...], parity_ref[...].astype(F32))
    stacked = jnp.concatenate([parts[:, :128], parts[:, 128:]], axis=0)
    native = exact(order_ref[...].astype(F32), stacked)
    native_ref[...] = native
    row = lax.broadcasted_iota(jnp.int32, (16, 128), 0)
    lane = lanes_of((16, 128))
    first = jnp.where((lane == row) & (row < EDGE), 1.0, 0.0).astype(F32)
    last = jnp.where((lane == row + 128 - EDGE) & (row < EDGE), 1.0, 0.0).astype(F32)
    over_lanes = (((1,), (1,)), ((), ()))
    left = exact(first, native, over_lanes)
    right = exact(last, native, over_lanes)
    same_ref[...] = jnp.where(core == 0, right, left)
    cross_ref[...] = jnp.where(core == 0, left, right)


def emit_messages(q_ref, coarse_ref, left_ref, right_ref, down_ref, up_ref):
    low = lax.broadcasted_iota(jnp.int32, (8, 128), 0) < 4
    for zc in range(4):
        means = []
        for xc in range(4):
            t = (q_ref[2 * zc, 2 * xc] + q_ref[2 * zc, 2 * xc + 1]) + (
                q_ref[2 * zc + 1, 2 * xc] + q_ref[2 * zc + 1, 2 * xc + 1]
            )
            means.append((t + pltpu.roll(t, 4, 0)) * 0.125)
        slab = jnp.concatenate(
            [jnp.where(low, means[0], means[1]), jnp.where(low, means[2], means[3])], axis=0
        ).astype(BF16)
        coarse_ref[pl.ds(zc * 16, 16), :] = slab
        left_ref[pl.ds(zc * 16, 16), :] = slab
        right_ref[pl.ds(zc * 16, 16), :] = slab
    for z in range(0, 8, 2):
        at = pl.ds(64 + z * 8, 16)
        left_ref[at, :] = jnp.concatenate([q_ref[z, 0], q_ref[z + 1, 0]], axis=0).astype(BF16)
        right_ref[at, :] = jnp.concatenate([q_ref[z, 7], q_ref[z + 1, 7]], axis=0).astype(BF16)
    for x in range(0, 8, 2):
        at = pl.ds(x * 8, 16)
        down_ref[at, :] = jnp.concatenate([q_ref[0, x], q_ref[0, x + 1]], axis=0).astype(BF16)
        up_ref[at, :] = jnp.concatenate([q_ref[7, x], q_ref[7, x + 1]], axis=0).astype(BF16)


MESSAGES = [((64, 128), BF16), ((128, 128), BF16), ((128, 128), BF16), ((64, 128), BF16), ((64, 128), BF16)]


def assemble_kernel(
    core_ref, own_ref, other_ref, same_ref, cross_ref, q_ref, coarse_ref, left_ref, right_ref, down_ref, up_ref
):
    core = core_ref[0]
    row = lax.broadcasted_iota(jnp.int32, (16, 128), 0)
    lane16 = lanes_of((16, 128))
    start = jnp.where(core == 0, 0, HALF + EDGE)
    place = jnp.where((lane16 == row + start) & (row < EDGE), 1.0, 0.0).astype(F32)
    lane = lanes_of((256, 128))
    begin = jnp.where(core == 0, EDGE, 0)
    inside = (lane >= begin) & (lane < begin + HALF + EDGE)
    shift = jnp.where(core == 0, EDGE, HALF + EDGE)
    over_rows = (((0,), (0,)), ((), ()))
    for block_ref, edge_ref, position in ((own_ref, same_ref, core), (other_ref, cross_ref, 1 - core)):
        edge = exact(edge_ref[...], place, over_rows)
        block = jnp.where(inside, pltpu.roll(block_ref[...], shift, 1), edge)
        q_ref[:, pl.ds(position * 4, 4)] = block.reshape(8, 4, 8, 128)
    emit_messages(q_ref, coarse_ref, left_ref, right_ref, down_ref, up_ref)


def weights_kernel(w1_ref, w2_ref, place1_ref, place2_ref, band1_ref, band2_ref):
    spread1 = jnp.dot(w1_ref[...], place1_ref[...], preferred_element_type=F32).astype(BF16)
    for xo in range(8):
        band1_ref[pl.ds(xo * 32, 32), :] = spread1[:, xo * 512 : (xo + 1) * 512]
    spread2 = jnp.dot(w2_ref[...], place2_ref[...], preferred_element_type=F32).astype(BF16)
    for xo in range(6):
        band2_ref[pl.ds(xo * 80, 80), :] = spread2[:, xo * 256 : (xo + 1) * 256]


def stage_body(
    q_ref, coarse_ref, from_left_ref, from_right_ref, below_ref, above_ref,
    band1_ref, band2_ref, bias_ref, div_ref, columns, parts, stress, update, new_ref,
):
    for j in range(10):
        if j < 3:
            ref, starts = below_ref, (j * 16, 48 + j * 16, 96 + j * 16)
            pieces = [ref[pl.ds(s, 16), :] for s in starts]
        elif j >= 7:
            ref, starts = above_ref, ((j - 7) * 16, 48 + (j - 7) * 16, 96 + (j - 7) * 16)
            pieces = [ref[pl.ds(s, 16), :] for s in starts]
        else:
            at = pl.ds((j - 3) * 16, 16)
            pieces = [from_left_ref[at, :], coarse_ref[at, :], from_right_ref[at, :]]
        for i, piece in enumerate(pieces):
            wide = piece.astype(F32)
            columns[pl.ds(j * 144 + i * 16, 16), :] = pltpu.roll(wide, 1, 1).astype(BF16)
            columns[pl.ds(j * 144 + 48 + i * 16, 16), :] = piece
            columns[pl.ds(j * 144 + 96 + i * 16, 16), :] = pltpu.roll(wide, 127, 1).astype(BF16)

    bias = jnp.concatenate([bias_ref[...]] * 8, axis=0)

    def layer(j, carry):
        rows = columns[pl.ds(pl.multiple_of(j * 144, 16), 432), :]
        pre = jnp.dot(band1_ref[:, :432], rows, preferred_element_type=F32) + bias
        inner = pre * (0.7978845608028654 + 0.7978845608028654 * 0.044715 * (pre * pre))
        half = 0.5 * pre
        hidden = (half + half * jnp.tanh(inner)).astype(BF16)
        parts[j] = jnp.dot(band2_ref[...], hidden, preferred_element_type=F32)
        return carry

    lax.fori_loop(0, 8, layer, 0, unroll=True)

    for k in range(6):
        rows = []
        for xo in range(6):
            sums = []
            for dy in range(3):
                at = [pl.ds(xo * 80 + (dz * 3 + dy) * 8, 8) for dz in range(3)]
                sums.append(parts[k, at[0], :] + parts[k + 1, at[1], :] + parts[k + 2, at[2], :])
            rows.append(sums[1] + pltpu.roll(sums[0], 1, 1) + pltpu.roll(sums[2], 127, 1))
        tile = jnp.concatenate(rows, axis=0).astype(BF16)
        stress[pl.ds(k * 48, 48), :] = tile
    low = lax.broadcasted_iota(jnp.int32, (8, 128), 0) < 4
    forces = []
    for k in range(1, 5):
        here = stress[pl.ds(k * 48, 48), :]
        wide = here.astype(F32)
        operand = jnp.concatenate(
            [
                stress[pl.ds((k - 1) * 48, 144), :],
                pltpu.roll(wide, 1, 1).astype(BF16),
                pltpu.roll(wide, 127, 1).astype(BF16),
            ],
            axis=0,
        )
        forces.append(jnp.dot(div_ref[...], operand, preferred_element_type=F32))

    below = [below_ref[pl.ds(144 + x * 8, 16), :].astype(F32) for x in range(0, 8, 2)]
    above = [above_ref[pl.ds(144 + x * 8, 16), :].astype(F32) for x in range(0, 8, 2)]
    left = [from_left_ref[pl.ds(64 + z * 8, 16), :].astype(F32) for z in range(0, 8, 2)]
    right = [from_right_ref[pl.ds(64 + z * 8, 16), :].astype(F32) for z in range(0, 8, 2)]

    def cell(z, x):
        if z < 0:
            return below[x // 2][(x % 2) * 8 : (x % 2) * 8 + 8]
        if z > 7:
            return above[x // 2][(x % 2) * 8 : (x % 2) * 8 + 8]
        if x < 0:
            return left[z // 2][(z % 2) * 8 : (z % 2) * 8 + 8]
        if x > 7:
            return right[z // 2][(z % 2) * 8 : (z % 2) * 8 + 8]
        return q_ref[z, x]

    for z in range(8):
        for x in range(8):
            here = q_ref[z, x]
            zp, zm, xp, xm = cell(z + 1, x), cell(z - 1, x), cell(z, x + 1), cell(z, x - 1)
            swap = pltpu.roll(here, 4, 0)
            back, ahead = pltpu.roll(swap, 1, 1), pltpu.roll(swap, 127, 1)
            far = jnp.where(low, back, ahead)
            slope_y = jnp.where(low, swap - back, ahead - swap)
            spread = (zp + zm) + (xp + xm) + (swap + far) - 6.0 * here

            def velocity(c):
                first = jnp.broadcast_to(q_ref[z, x, c : c + 1, :], (8, 128))
                second = jnp.broadcast_to(q_ref[z, x, c + 4 : c + 5, :], (8, 128))
                return jnp.where(low, first, second)

            advect = velocity(0) * (xp - xm) + velocity(1) * slope_y + velocity(2) * (zp - zm)
            force = forces[z // 2][(x // 2) * 8 : (x // 2) * 8 + 8]
            rate = viscosity * spread - 0.5 * advect + force
            new_ref[z, x] = update(z, x, here, rate)


def stage1_kernel(*refs):
    ins, outs, (columns, parts, stress) = refs[:10], refs[10:16], refs[16:]
    stage_body(*ins, columns, parts, stress, lambda z, x, q, r: q + time_step * r, outs[0])
    emit_messages(*outs)


def stage2_kernel(base_ref, *refs):
    ins, outs, (columns, parts, stress) = refs[:10], refs[10:16], refs[16:]

    def update(z, x, q, r):
        return 0.75 * base_ref[z, x] + 0.25 * (q + time_step * r)

    stage_body(*ins, columns, parts, stress, update, outs[0])
    emit_messages(*outs)


def stage3_kernel(core_ref, base_ref, *refs):
    ins, outs, (columns, parts, stress, new) = refs[:10], refs[10:12], refs[12:]
    core = core_ref[0]

    def update(z, x, q, r):
        return base_ref[z, x] * (1.0 / 3.0) + (2.0 / 3.0) * (q + time_step * r)

    stage_body(*ins, columns, parts, stress, update, new)
    outs[0][...] = new[:, pl.ds(core * 4, 4)]
    outs[1][...] = new[:, pl.ds((1 - core) * 4, 4)]


def finish_kernel(core_ref, own_ref, other_ref, parity_ref, order_ref, out_ref, flat):
    core = core_ref[0]
    lane = lanes_of((256, 128))
    own = own_ref[...].reshape(256, 128)
    other = other_ref[...].reshape(256, 128)
    low = jnp.where(core == 0, own, other)
    high = jnp.where(core == 0, other, own)
    native = jnp.where(lane < HALF, pltpu.roll(low, 128 - EDGE, 1), pltpu.roll(high, HALF - EDGE, 1))
    stacked = exact(order_ref[...].astype(F32), native, (((0,), (0,)), ((), ())))
    parts = jnp.concatenate([stacked[:128], stacked[128:]], axis=1)
    flat[...] = exact(parts, parity_ref[...].astype(F32), (((1,), (1,)), ((), ())))
    for c in range(4):
        for z in range(8):
            out_ref[c, z] = flat[pl.ds((c * 8 + z) * 4, 4), :]


def chip_shift(value, step):
    size = lax.axis_size("wide")
    return lax.ppermute(value, "wide", [(i, (i + 2 * step) % size) for i in range(size)])


def net_shift(value, step):
    size = lax.axis_size("net")
    return lax.ppermute(value, "net", [(i, (i + step) % size) for i in range(size)])


def partner(value):
    return lax.ppermute(value, "wide", [(i, i ^ 1) for i in range(lax.axis_size("wide"))])


def edge_shift(value, cross):
    wide, narrow = lax.axis_size("wide"), lax.axis_size("narrow")
    pairs = []
    for w in range(wide):
        for r in range(narrow):
            if cross:
                step, to = (-1 if w % 2 == 0 else 1), w ^ 1
            else:
                step, to = (1 if w % 2 == 0 else -1), w
            pairs.append((w * narrow + r, to * narrow + (r + step) % narrow))
    return lax.ppermute(value, ("wide", "narrow"), pairs)


def per_device(fields, conv1_weight, conv1_bias, conv2_weight):
    core = (lax.axis_index("wide") % 2).astype(jnp.int32).reshape(1)
    parity = jnp.asarray(split_parity(), BF16)
    order = jnp.asarray(row_order(), BF16)
    native, same, cross = call(
        pack_kernel,
        [((256, 128), F32), ((16, 256), F32), ((16, 256), F32)],
        [pltpu.VMEM((128, 256), F32)],
        core, fields, parity, order,
    )
    other = partner(native)
    same = edge_shift(same, False)
    cross = edge_shift(cross, True)

    w1 = conv1_weight.transpose(1, 0, 2).reshape(32, 108)
    w2 = conv2_weight.reshape(3, 3, 3, 6, 32).transpose(0, 2, 3, 1, 4)
    w2 = jnp.pad(w2, ((0, 0), (0, 0), (0, 2), (0, 0), (0, 0))).reshape(72, 96)
    w2 = jnp.pad(w2, ((0, 8), (0, 0)))
    bias = jnp.broadcast_to(conv1_bias[:, None], (32, 128))
    band1, band2 = call(
        weights_kernel,
        [((256, 512), BF16), ((480, 256), BF16)],
        [],
        w1, w2, jnp.asarray(place_conv1(), BF16), jnp.asarray(place_conv2(), BF16),
    )
    fixed = (band1, band2, bias, jnp.asarray(divergence_matrix(), BF16))

    base, *messages = call(
        assemble_kernel, [((8, 8, 8, 128), F32)] + MESSAGES, [], core, native, other, same, cross
    )
    scratch = [
        pltpu.VMEM((1440, 128), BF16),
        pltpu.VMEM((8, 480, 128), F32),
        pltpu.VMEM((288, 128), BF16),
    ]

    def exchange(coarse, to_left, to_right, down, up):
        from_left, from_right = chip_shift(to_right, 1), chip_shift(to_left, -1)
        going_up = jnp.concatenate([from_left[16:64], coarse[16:64], from_right[16:64], up], axis=0)
        going_down = jnp.concatenate([from_left[:48], coarse[:48], from_right[:48], down], axis=0)
        below, above = net_shift(going_up, 1), net_shift(going_down, -1)
        return coarse, from_left, from_right, below, above

    state_out = [((8, 8, 8, 128), F32)] + MESSAGES
    one, *messages = call(stage1_kernel, state_out, scratch, base, *exchange(*messages), *fixed)
    two, *messages = call(stage2_kernel, state_out, scratch, base, one, *exchange(*messages), *fixed)
    own, away = call(
        stage3_kernel,
        [((8, 4, 8, 128), F32)] * 2,
        scratch + [pltpu.VMEM((8, 8, 8, 128), F32)],
        core, base, two, *exchange(*messages), *fixed,
    )
    back = partner(away)
    (out,) = call(
        finish_kernel,
        [(fields.shape, F32)],
        [pltpu.VMEM((128, 256), F32)],
        core, own, back, parity, order,
    )
    return out


def solution(mesh):
    in_specs = (P(None, "net", "wide", "narrow"), P(), P(), P())
    out_specs = P(None, "net", "wide", "narrow")
    return jax.shard_map(
        per_device, mesh=mesh, in_specs=in_specs, out_specs=out_specs, check_vma=False
    )
```

```python
import jax
import jax.numpy as jnp
import numpy as np
from jax import lax
from jax.experimental import pallas as pl
from jax.experimental.pallas import tpu as pltpu
from jax.sharding import PartitionSpec as P

time_step = 0.2
viscosity = 0.05
EDGE = 9
HALF = 64
F32 = jnp.float32
BF16 = jnp.bfloat16
VM = pl.BlockSpec(memory_space=pltpu.VMEM)
SM = pl.BlockSpec(memory_space=pltpu.SMEM)


def split_parity():
    m = np.zeros((256, 256), np.float32)
    for l in range(128):
        m[2 * l, l] = 1.0
        m[2 * l + 1, 128 + l] = 1.0
    return m


def divergence_matrix():
    m = np.zeros((4, 2, 4, 5, 6, 8), np.float32)
    sx, sy, sz = (0, 3, 4), (3, 1, 5), (4, 5, 2)
    for x in range(4):
        for comp in range(3):
            m[x, :, comp, 1, x + 2, sx[comp]] += 0.25
            m[x, :, comp, 1, x, sx[comp]] -= 0.25
            m[x, :, comp, 4, x + 1, sy[comp]] += 0.25
            m[x, :, comp, 3, x + 1, sy[comp]] -= 0.25
            m[x, :, comp, 2, x + 1, sz[comp]] += 0.25
            m[x, :, comp, 0, x + 1, sz[comp]] -= 0.25
    return m.reshape(32, 240)


def near(value):
    return pltpu.with_memory_space_constraint(value, pltpu.VMEM)


def call(kernel, outs, scratch, info, *args, result=None):
    return pl.pallas_call(
        kernel,
        out_shape=result or [pltpu.VMEM(s, d) for s, d in outs],
        in_specs=[SM] + [VM] * len(args),
        out_specs=VM if result else [VM] * len(outs),
        scratch_shapes=scratch,
    )(info, *args)


def lanes_of(shape):
    return lax.broadcasted_iota(jnp.int32, shape, len(shape) - 1)


def thirds(value):
    first = value.astype(BF16)
    rest = value - first.astype(F32)
    second = rest.astype(BF16)
    third = (rest - second.astype(F32)).astype(BF16)
    return jnp.concatenate([first, second, third], axis=0)


def pack_kernel(info_ref, fields_ref, parity_ref, native_ref, same_ref, cross_ref, flat):
    core = info_ref[0]
    for c in range(4):
        for z in range(8):
            flat[pl.ds((c * 8 + z) * 4, 4), :] = fields_ref[c, z]
    split = jnp.dot(thirds(flat[...]), parity_ref[...], preferred_element_type=F32)
    parts = split[:128] + split[128:256] + split[256:]
    for p in range(2):
        for c in range(4):
            native_ref[pl.ds(p * 4 + c, 32, stride=8), :] = parts[
                c * 32 : (c + 1) * 32, p * 128 : (p + 1) * 128
            ]
    lane = lanes_of((32, 128))
    for out_ref, take_last in ((same_ref, core == 0), (cross_ref, core == 1)):
        offset = jnp.where(take_last, EDGE, 0)
        total = jnp.zeros((32, 128), F32)
        for g in range(8):
            moved = pltpu.roll(native_ref[pl.ds(g * 32, 32), :], g * 16 + offset, 1)
            total = jnp.where((lane >= g * 16) & (lane < g * 16 + EDGE), moved, total)
        out_ref[...] = total


def emit_messages(info_ref, q_ref, wide_a_ref, wide_b_ref, net_a_ref, net_b_ref):
    chip_even, net_even = info_ref[1] == 0, info_ref[2] == 0
    low = lax.broadcasted_iota(jnp.int32, (8, 128), 0) < 4
    slabs = []
    for zc in range(4):
        means = []
        for xc in range(4):
            t = (q_ref[2 * zc, 2 * xc] + q_ref[2 * zc, 2 * xc + 1]) + (
                q_ref[2 * zc + 1, 2 * xc] + q_ref[2 * zc + 1, 2 * xc + 1]
            )
            means.append((t + pltpu.roll(t, 4, 0)) * 0.125)
        slab = jnp.concatenate(
            [jnp.where(low, means[0], means[1]), jnp.where(low, means[2], means[3])], axis=0
        )
        slabs.append(slab)
        wide_a_ref[pl.ds(zc * 16, 16), :] = slab.astype(BF16)
        wide_b_ref[pl.ds(zc * 16, 16), :] = slab.astype(BF16)
    for zc in range(3):
        at = pl.ds(zc * 16, 16)
        net_a_ref[at, :] = jnp.where(net_even, slabs[zc + 1], slabs[zc]).astype(BF16)
        net_b_ref[at, :] = jnp.where(net_even, slabs[zc], slabs[zc + 1]).astype(BF16)
    xa, xb = jnp.where(chip_even, 7, 0), jnp.where(chip_even, 0, 7)
    za, zb = jnp.where(net_even, 7, 0), jnp.where(net_even, 0, 7)
    for z in range(0, 8, 2):
        at = pl.ds(64 + z * 8, 16)
        wide_a_ref[at, :] = jnp.concatenate([q_ref[z, xa], q_ref[z + 1, xa]], axis=0).astype(BF16)
        wide_b_ref[at, :] = jnp.concatenate([q_ref[z, xb], q_ref[z + 1, xb]], axis=0).astype(BF16)
    for x in range(0, 8, 2):
        at = pl.ds(48 + x * 8, 16)
        net_a_ref[at, :] = jnp.concatenate([q_ref[za, x], q_ref[za, x + 1]], axis=0).astype(BF16)
        net_b_ref[at, :] = jnp.concatenate([q_ref[zb, x], q_ref[zb, x + 1]], axis=0).astype(BF16)


MESSAGES = [((128, 128), BF16), ((128, 128), BF16), ((112, 128), BF16), ((112, 128), BF16)]


def assemble_kernel(
    info_ref, own_ref, other_ref, same_ref, cross_ref, q_ref, wide_a_ref, wide_b_ref, net_a_ref, net_b_ref
):
    core = info_ref[0]
    lane = lanes_of((32, 128))
    begin = jnp.where(core == 0, EDGE, 0)
    inside = (lane >= begin) & (lane < begin + HALF + EDGE)
    shift = jnp.where(core == 0, EDGE, HALF + EDGE)
    start = jnp.where(core == 0, 128, HALF + EDGE + 128)
    for block_ref, edge_ref, position in ((own_ref, same_ref, core), (other_ref, cross_ref, 1 - core)):
        edge = edge_ref[...]
        for g in range(8):
            block = pltpu.roll(block_ref[pl.ds(g * 32, 32), :], shift, 1)
            block = jnp.where(inside, block, pltpu.roll(edge, lax.rem(start - g * 16, 128), 1))
            q_ref[g, pl.ds(position * 4, 4)] = block.reshape(4, 8, 128)
    emit_messages(info_ref, q_ref, wide_a_ref, wide_b_ref, net_a_ref, net_b_ref)


def weights_kernel(info_ref, w1_ref, w2_ref, b_ref, band1_ref, band2_ref, bias_ref, flat1, flat2):
    flat1[...] = jnp.zeros_like(flat1)
    flat2[...] = jnp.zeros_like(flat2)
    for dz in range(3):
        for dx in range(3):
            for dy in range(3):
                tap = 9 * dz + 3 * dx + dy
                flat1[:, pl.ds((dz * 3 + dy) * 48 + (1 + dx) * 4, 4)] = w1_ref[tap].astype(F32)
                flat2[pl.ds((dz * 3 + dy) * 8, 6), pl.ds(dx * 32, 32)] = w2_ref[tap].astype(F32)
    for xo in range(8):
        band1_ref[pl.ds(xo * 32, 32), :] = pltpu.roll(flat1[...], 4 * xo, 1).astype(BF16)
    for xo in range(6):
        band2_ref[pl.ds(xo * 80, 80), :] = pltpu.roll(flat2[...], 32 * xo, 1).astype(BF16)
    square = jnp.broadcast_to(b_ref[...], (32, 32))
    diagonal = lanes_of((32, 32)) == lax.broadcasted_iota(jnp.int32, (32, 32), 0)
    column = jnp.sum(jnp.where(diagonal, square, 0.0), axis=1, keepdims=True)
    bias_ref[...] = jnp.broadcast_to(column, (32, 128))


def stage_body(
    info_ref, q_ref, coarse_ref, wide_a_ref, wide_b_ref, net_a_ref, net_b_ref,
    band1_ref, band2_ref, bias_ref, div_ref, columns, parts, stress, update, new_ref,
):
    chip_even = info_ref[1] == 0
    net_even = info_ref[2] == 0
    left_at, right_at = jnp.where(chip_even, 160, 112), jnp.where(chip_even, 112, 160)

    def slab(j, pieces):
        for i, piece in enumerate(pieces):
            wide = piece.astype(F32)
            columns[pl.ds(j * 144 + i * 16, 16), :] = pltpu.roll(wide, 1, 1).astype(BF16)
            columns[pl.ds(j * 144 + 48 + i * 16, 16), :] = wide.astype(BF16)
            columns[pl.ds(j * 144 + 96 + i * 16, 16), :] = pltpu.roll(wide, 127, 1).astype(BF16)

    def wide_rows(start):
        a = wide_a_ref[pl.ds(start, 16), :].astype(F32)
        b = wide_b_ref[pl.ds(start, 16), :].astype(F32)
        return jnp.where(chip_even, b, a), jnp.where(chip_even, a, b)

    def net_rows(start):
        a = net_a_ref[pl.ds(start, 16), :].astype(F32)
        b = net_b_ref[pl.ds(start, 16), :].astype(F32)
        return jnp.where(net_even, b, a), jnp.where(net_even, a, b)

    bias = jnp.concatenate([bias_ref[...]] * 8, axis=0)
    bias = jnp.concatenate([bias, bias], axis=1)

    def layers(j, k):
        rows = jnp.concatenate(
            [columns[pl.ds(j * 144, 432), :], columns[pl.ds(k * 144, 432), :]], axis=1
        )
        pre = jnp.dot(band1_ref[:, :432], rows, preferred_element_type=F32) + bias
        inner = pre * (0.7978845608028654 + 0.7978845608028654 * 0.044715 * (pre * pre))
        half = 0.5 * pre
        hidden = (half + half * jnp.tanh(inner)).astype(BF16)
        both = jnp.dot(band2_ref[...], hidden, preferred_element_type=F32)
        parts[j] = both[:, :128]
        parts[k] = both[:, 128:]

    for j in range(3, 7):
        at = (j - 3) * 16
        left, right = wide_rows(at)
        slab(j, [left, coarse_ref[pl.ds(at, 16), :], right])
    layers(3, 4)
    for i in range(3):
        starts = [pl.multiple_of(at + i * 16, 16) for at in (left_at, 0, right_at)]
        below, above = zip(*[net_rows(start) for start in starts])
        slab(i, below)
        slab(7 + i, above)
    layers(1, 2)
    layers(5, 6)
    layers(0, 7)

    for k in range(6):
        rows = []
        for xo in range(6):
            sums = []
            for dy in range(3):
                at = [pl.ds(xo * 80 + (dz * 3 + dy) * 8, 8) for dz in range(3)]
                sums.append(parts[k, at[0], :] + parts[k + 1, at[1], :] + parts[k + 2, at[2], :])
            rows.append(sums[1] + pltpu.roll(sums[0], 1, 1) + pltpu.roll(sums[2], 127, 1))
        stress[pl.ds(k * 48, 48), :] = jnp.concatenate(rows, axis=0).astype(BF16)
    low = lax.broadcasted_iota(jnp.int32, (8, 128), 0) < 4
    forces = []
    for k in range(1, 5, 2):
        operands = []
        for m in (k, k + 1):
            wide = stress[pl.ds(m * 48, 48), :].astype(F32)
            operands.append(
                jnp.concatenate(
                    [
                        stress[pl.ds((m - 1) * 48, 144), :],
                        pltpu.roll(wide, 1, 1).astype(BF16),
                        pltpu.roll(wide, 127, 1).astype(BF16),
                    ],
                    axis=0,
                )
            )
        both = jnp.dot(
            div_ref[...], jnp.concatenate(operands, axis=1), preferred_element_type=F32
        )
        forces += [both[:, :128], both[:, 128:]]

    below, above = zip(*[net_rows(48 + x * 8) for x in range(0, 8, 2)])
    left, right = zip(*[wide_rows(64 + z * 8) for z in range(0, 8, 2)])

    def half_of(pair, i):
        return pair[i // 2][(i % 2) * 8 : (i % 2) * 8 + 8]

    def cell(z, x):
        if z < 0:
            return half_of(below, x)
        if z > 7:
            return half_of(above, x)
        if x < 0:
            return half_of(left, z)
        if x > 7:
            return half_of(right, z)
        return q_ref[z, x]

    for z in range(8):
        for x in range(8):
            here = q_ref[z, x]
            zp, zm, xp, xm = cell(z + 1, x), cell(z - 1, x), cell(z, x + 1), cell(z, x - 1)
            swap = pltpu.roll(here, 4, 0)
            back, ahead = pltpu.roll(swap, 1, 1), pltpu.roll(swap, 127, 1)
            far = jnp.where(low, back, ahead)
            slope_y = jnp.where(low, swap - back, ahead - swap)
            spread = (zp + zm) + (xp + xm) + (swap + far) - 6.0 * here

            def velocity(c):
                first = jnp.broadcast_to(q_ref[z, x, c : c + 1, :], (8, 128))
                second = jnp.broadcast_to(q_ref[z, x, c + 4 : c + 5, :], (8, 128))
                return jnp.where(low, first, second)

            advect = velocity(0) * (xp - xm) + velocity(1) * slope_y + velocity(2) * (zp - zm)
            force = forces[z // 2][(x // 2) * 8 : (x // 2) * 8 + 8]
            rate = viscosity * spread - 0.5 * advect + force
            new_ref[z, x] = update(z, x, here, rate)


def stage1_kernel(*refs):
    ins, outs, scratch = refs[:11], refs[11:16], refs[16:]
    stage_body(*ins, *scratch, lambda z, x, q, r: q + time_step * r, outs[0])
    emit_messages(ins[0], *outs)


def stage2_kernel(*refs):
    ins, base_ref, outs, scratch = refs[:11], refs[11], refs[12:17], refs[17:]

    def update(z, x, q, r):
        return 0.75 * base_ref[z, x] + 0.25 * (q + time_step * r)

    stage_body(*ins, *scratch, update, outs[0])
    emit_messages(ins[0], *outs)


def stage3_kernel(*refs):
    ins, base_ref, outs, scratch, new = refs[:11], refs[11], refs[12:14], refs[14:-1], refs[-1]
    core = ins[0][0]

    def update(z, x, q, r):
        return base_ref[z, x] * (1.0 / 3.0) + (2.0 / 3.0) * (q + time_step * r)

    stage_body(*ins, *scratch, update, new)
    outs[0][...] = new[:, pl.ds(core * 4, 4)].reshape(256, 128)
    outs[1][...] = new[:, pl.ds((1 - core) * 4, 4)].reshape(256, 128)


def finish_kernel(info_ref, own_ref, other_ref, parity_ref, out_ref, native, flat):
    core = info_ref[0]
    lane = lanes_of((256, 128))
    low = jnp.where(core == 0, own_ref[...], other_ref[...])
    high = jnp.where(core == 0, other_ref[...], own_ref[...])
    native[...] = jnp.where(
        lane < HALF, pltpu.roll(low, 128 - EDGE, 1), pltpu.roll(high, HALF - EDGE, 1)
    )
    halves = [
        jnp.concatenate([native[pl.ds(p * 4 + c, 32, stride=8), :] for c in range(4)], axis=0)
        for p in range(2)
    ]
    split = lax.dot_general(
        thirds(jnp.concatenate(halves, axis=1)),
        parity_ref[...],
        (((1,), (1,)), ((), ())),
        preferred_element_type=F32,
    )
    flat[...] = split[:128] + split[128:256] + split[256:]
    for c in range(4):
        for z in range(8):
            out_ref[c, z] = flat[pl.ds((c * 8 + z) * 4, 4), :]


def chip_swap(value, odd):
    size = lax.axis_size("wide")
    pairs = []
    for i in range(size):
        chip, core = divmod(i, 2)
        to = chip + 1 if (chip + odd) % 2 == 0 else chip - 1
        pairs.append((i, (2 * to + core) % size))
    return lax.ppermute(value, "wide", pairs)


def net_swap(value, odd):
    size = lax.axis_size("net")
    pairs = [(i, (i + 1 if (i + odd) % 2 == 0 else i - 1) % size) for i in range(size)]
    return lax.ppermute(value, "net", pairs)


def partner(value):
    return lax.ppermute(value, "wide", [(i, i ^ 1) for i in range(lax.axis_size("wide"))])


def edge_shift(value, cross):
    wide, narrow = lax.axis_size("wide"), lax.axis_size("narrow")
    pairs = []
    for w in range(wide):
        for r in range(narrow):
            if cross:
                step, to = (-1 if w % 2 == 0 else 1), w ^ 1
            else:
                step, to = (1 if w % 2 == 0 else -1), w
            pairs.append((w * narrow + r, to * narrow + (r + step) % narrow))
    return lax.ppermute(value, ("wide", "narrow"), pairs)


def per_device(fields, conv1_weight, conv1_bias, conv2_weight):
    wide, net = lax.axis_index("wide"), lax.axis_index("net")
    info = jnp.stack([wide % 2, (wide // 2) % 2, net % 2]).astype(jnp.int32)
    parity = near(jnp.asarray(split_parity(), BF16))
    native, same, cross = call(
        pack_kernel,
        [((256, 128), F32), ((32, 128), F32), ((32, 128), F32)],
        [pltpu.VMEM((128, 256), F32)],
        info, fields, parity,
    )
    other = near(partner(native))
    same = near(edge_shift(same, False))
    cross = near(edge_shift(cross, True))
    fixed = call(
        weights_kernel,
        [((256, 512), BF16), ((480, 256), BF16), ((32, 128), F32)],
        [pltpu.VMEM((32, 512), F32), pltpu.VMEM((80, 256), F32)],
        info, conv1_weight, conv2_weight, conv1_bias.reshape(1, 32),
    )
    fixed = (*map(near, fixed), near(jnp.asarray(divergence_matrix(), BF16)))
    base, *messages = call(
        assemble_kernel,
        [((8, 8, 8, 128), F32)] + MESSAGES,
        [],
        info, near(native), other, same, cross,
    )
    base = near(base)
    scratch = [
        pltpu.VMEM((1440, 128), BF16),
        pltpu.VMEM((8, 480, 128), F32),
        pltpu.VMEM((288, 128), BF16),
    ]
    even = net % 2 == 0

    def exchange(wide_a, wide_b, net_a, net_b):
        got_a, got_b = chip_swap(wide_a, 0), chip_swap(wide_b, 1)
        rows_a = [jnp.where(even, got[16:64], got[:48]) for got in (got_a, got_b)]
        rows_b = [jnp.where(even, got[:48], got[16:64]) for got in (got_a, got_b)]
        far_a = net_swap(jnp.concatenate([net_a, *rows_a], axis=0), 0)
        far_b = net_swap(jnp.concatenate([net_b, *rows_b], axis=0), 1)
        return map(near, (wide_a, got_a, got_b, far_a, far_b))

    state_out = [((8, 8, 8, 128), F32)] + MESSAGES
    one, *messages = call(
        stage1_kernel, state_out, scratch, info, base, *exchange(*messages), *fixed
    )
    two, *messages = call(
        stage2_kernel, state_out, scratch, info, near(one), *exchange(*messages), *fixed, base
    )
    own, away = call(
        stage3_kernel,
        [((256, 128), F32)] * 2,
        scratch + [pltpu.VMEM((8, 8, 8, 128), F32)],
        info, near(two), *exchange(*messages), *fixed, base,
    )
    return call(
        finish_kernel,
        None,
        [pltpu.VMEM((256, 128), F32), pltpu.VMEM((128, 256), F32)],
        info, near(own), near(partner(away)), parity,
        result=jax.ShapeDtypeStruct(fields.shape, F32),
    )


def solution(mesh):
    in_specs = (P(None, "net", "wide", "narrow"), P(), P(), P())
    out_specs = P(None, "net", "wide", "narrow")
    return jax.shard_map(
        per_device, mesh=mesh, in_specs=in_specs, out_specs=out_specs, check_vma=False
    )
```

```python
import functools

import jax
import jax.numpy as jnp
import numpy as np
from jax import lax
from jax.experimental import pallas as pl
from jax.experimental.pallas import tpu as pltpu
from jax.sharding import PartitionSpec as P

time_step = 0.2
viscosity = 0.05
EDGE = 9
HALF = 64
VMEM_LIMIT = 16 << 20
F32 = jnp.float32
BF16 = jnp.bfloat16
VM = pl.BlockSpec(memory_space=pltpu.VMEM)
SM = pl.BlockSpec(memory_space=pltpu.SMEM)


def divergence_matrix():
    m = np.zeros((4, 2, 4, 5, 6, 8), np.float32)
    sx, sy, sz = (0, 3, 4), (3, 1, 5), (4, 5, 2)
    for x in range(4):
        for comp in range(3):
            m[x, :, comp, 1, x + 2, sx[comp]] += 0.25
            m[x, :, comp, 1, x, sx[comp]] -= 0.25
            m[x, :, comp, 4, x + 1, sy[comp]] += 0.25
            m[x, :, comp, 3, x + 1, sy[comp]] -= 0.25
            m[x, :, comp, 2, x + 1, sz[comp]] += 0.25
            m[x, :, comp, 0, x + 1, sz[comp]] -= 0.25
    return m.reshape(32, 240)


def near(value):
    return pltpu.with_memory_space_constraint(value, pltpu.VMEM)


def call(kernel, outs, scratch, info, *args, result=None):
    return pl.pallas_call(
        kernel,
        out_shape=result or [pltpu.VMEM(s, d) for s, d in outs],
        in_specs=[SM] + [VM] * len(args),
        out_specs=VM if result else [VM] * len(outs),
        scratch_shapes=scratch,
        compiler_params=pltpu.CompilerParams(vmem_limit_bytes=VMEM_LIMIT),
    )(info, *args)


def lanes_of(shape):
    return lax.broadcasted_iota(jnp.int32, shape, len(shape) - 1)


def thirds(value):
    first = value.astype(BF16)
    rest = value - first.astype(F32)
    second = rest.astype(BF16)
    third = (rest - second.astype(F32)).astype(BF16)
    return jnp.concatenate([first, second, third], axis=0)


def pack_kernel(info_ref, fields_ref, native_ref, same_ref, cross_ref, parity_ref, flat):
    core = info_ref[0]
    row, col = lax.broadcasted_iota(jnp.int32, (256, 256), 0), lanes_of((256, 256))
    source = jnp.where(col < 128, 2 * col, 2 * col - 255)
    parity_ref[...] = jnp.where(row == source, 1.0, 0.0).astype(F32).astype(BF16)
    for c in range(4):
        for z in range(8):
            flat[pl.ds((c * 8 + z) * 4, 4), :] = fields_ref[c, z]
    split = jnp.dot(thirds(flat[...]), parity_ref[...], preferred_element_type=F32)
    parts = split[:128] + split[128:256] + split[256:]
    for p in range(2):
        for c in range(4):
            native_ref[pl.ds(p * 4 + c, 32, stride=8), :] = parts[
                c * 32 : (c + 1) * 32, p * 128 : (p + 1) * 128
            ]
    lane = lanes_of((32, 128))
    for out_ref, take_last in ((same_ref, core == 0), (cross_ref, core == 1)):
        offset = jnp.where(take_last, EDGE, 0)
        total = jnp.zeros((32, 128), F32)
        for g in range(8):
            moved = pltpu.roll(native_ref[pl.ds(g * 32, 32), :], g * 16 + offset, 1)
            total = jnp.where((lane >= g * 16) & (lane < g * 16 + EDGE), moved, total)
        out_ref[...] = total


def emit_messages(info_ref, q_ref, wide_a_ref, wide_b_ref, net_a_ref, net_b_ref):
    chip_even, net_even = info_ref[1] == 0, info_ref[2] == 0
    low = lax.broadcasted_iota(jnp.int32, (8, 128), 0) < 4
    slabs = []
    for zc in range(4):
        means = []
        for xc in range(4):
            t = (q_ref[2 * zc, 2 * xc] + q_ref[2 * zc, 2 * xc + 1]) + (
                q_ref[2 * zc + 1, 2 * xc] + q_ref[2 * zc + 1, 2 * xc + 1]
            )
            means.append((t + pltpu.roll(t, 4, 0)) * 0.125)
        slab = jnp.concatenate(
            [jnp.where(low, means[0], means[1]), jnp.where(low, means[2], means[3])], axis=0
        )
        slabs.append(slab)
        wide_a_ref[pl.ds(zc * 16, 16), :] = slab.astype(BF16)
        wide_b_ref[pl.ds(zc * 16, 16), :] = slab.astype(BF16)
    for zc in range(3):
        at = pl.ds(zc * 16, 16)
        net_a_ref[at, :] = jnp.where(net_even, slabs[zc + 1], slabs[zc]).astype(BF16)
        net_b_ref[at, :] = jnp.where(net_even, slabs[zc], slabs[zc + 1]).astype(BF16)
    xa, xb = jnp.where(chip_even, 7, 0), jnp.where(chip_even, 0, 7)
    za, zb = jnp.where(net_even, 7, 0), jnp.where(net_even, 0, 7)
    for z in range(0, 8, 2):
        at = pl.ds(64 + z * 8, 16)
        wide_a_ref[at, :] = jnp.concatenate([q_ref[z, xa], q_ref[z + 1, xa]], axis=0).astype(BF16)
        wide_b_ref[at, :] = jnp.concatenate([q_ref[z, xb], q_ref[z + 1, xb]], axis=0).astype(BF16)
    for x in range(0, 8, 2):
        at = pl.ds(48 + x * 8, 16)
        net_a_ref[at, :] = jnp.concatenate([q_ref[za, x], q_ref[za, x + 1]], axis=0).astype(BF16)
        net_b_ref[at, :] = jnp.concatenate([q_ref[zb, x], q_ref[zb, x + 1]], axis=0).astype(BF16)


MESSAGES = [((128, 128), BF16), ((128, 128), BF16), ((112, 128), BF16), ((112, 128), BF16)]


def assemble_kernel(
    info_ref, own_ref, other_ref, same_ref, cross_ref, ready_ref,
    q_ref, wide_a_ref, wide_b_ref, net_a_ref, net_b_ref,
):
    core = info_ref[0]
    lane = lanes_of((32, 128))
    begin = jnp.where(core == 0, EDGE, 0)
    inside = (lane >= begin) & (lane < begin + HALF + EDGE)
    shift = jnp.where(core == 0, EDGE, HALF + EDGE)
    start = jnp.where(core == 0, 128, HALF + EDGE + 128)
    for block_ref, edge_ref, position in ((own_ref, same_ref, core), (other_ref, cross_ref, 1 - core)):
        edge = edge_ref[...]
        for g in range(8):
            block = pltpu.roll(block_ref[pl.ds(g * 32, 32), :], shift, 1)
            block = jnp.where(inside, block, pltpu.roll(edge, lax.rem(start - g * 16, 128), 1))
            q_ref[g, pl.ds(position * 4, 4)] = block.reshape(4, 8, 128)
    emit_messages(info_ref, q_ref, wide_a_ref, wide_b_ref, net_a_ref, net_b_ref)


def weights_kernel(info_ref, w1_ref, w2_ref, b_ref, band1_ref, band2_ref, bias_ref, flat1, flat2, tall):
    flat1[...] = jnp.zeros_like(flat1)
    flat2[...] = jnp.zeros_like(flat2)
    for dz in range(3):
        for dx in range(3):
            for dy in range(3):
                tap = 9 * dz + 3 * dx + dy
                flat1[:, pl.ds((dz * 3 + dy) * 48 + (1 + dx) * 4, 4)] = w1_ref[tap].astype(F32)
                flat2[pl.ds((dz * 3 + dy) * 8, 6), pl.ds(dx * 32, 32)] = w2_ref[tap].astype(F32)
    for xo in range(8):
        band1_ref[pl.ds(xo * 32, 32), :] = pltpu.roll(flat1[...], 4 * xo, 1).astype(BF16)
    for xo in range(6):
        tall[pl.ds(xo * 72, 72), :] = pltpu.roll(flat2[...], 32 * xo, 1)
    band2_ref[...] = tall[...].astype(BF16)
    square = jnp.broadcast_to(b_ref[...], (32, 32))
    diagonal = lanes_of((32, 32)) == lax.broadcasted_iota(jnp.int32, (32, 32), 0)
    column = jnp.sum(jnp.where(diagonal, square, 0.0), axis=1, keepdims=True)
    bias_ref[...] = jnp.broadcast_to(column, (32, 128))


def slab(ref, start, pieces):
    for i, piece in enumerate(pieces):
        wide = piece.astype(F32)
        ref[pl.ds(start + i * 16, 16), :] = pltpu.roll(wide, 1, 1).astype(BF16)
        ref[pl.ds(start + 48 + i * 16, 16), :] = wide.astype(BF16)
        ref[pl.ds(start + 96 + i * 16, 16), :] = pltpu.roll(wide, 127, 1).astype(BF16)


def rows_of(even, a_ref, b_ref, start):
    a = a_ref[pl.ds(start, 16), :].astype(F32)
    b = b_ref[pl.ds(start, 16), :].astype(F32)
    return jnp.where(even, b, a), jnp.where(even, a, b)


def layers(first, second, band1_ref, band2_ref, bias_ref):
    rows = jnp.concatenate(
        [jnp.concatenate(first, axis=0), jnp.concatenate(second, axis=0)], axis=1
    )
    bias = jnp.concatenate([bias_ref[...]] * 8, axis=0)
    bias = jnp.concatenate([bias, bias], axis=1)
    pre = jnp.dot(band1_ref[:, :432], rows, preferred_element_type=F32) + bias
    inner = pre * (0.7978845608028654 + 0.7978845608028654 * 0.044715 * (pre * pre))
    half = 0.5 * pre
    hidden = (half + half * jnp.tanh(inner)).astype(BF16)
    both = jnp.dot(band2_ref[...], hidden, preferred_element_type=F32)
    return both[:, :128], both[:, 128:]


def half_of(pair, i):
    return pair[i // 2][(i % 2) * 8 : (i % 2) * 8 + 8]


def velocity(q_ref, z, x, c, low):
    first = jnp.broadcast_to(q_ref[z, x, c : c + 1, :], (8, 128))
    second = jnp.broadcast_to(q_ref[z, x, c + 4 : c + 5, :], (8, 128))
    return jnp.where(low, first, second)


def before_kernel(weights, *refs):
    keep_base, keep_state, step = weights
    info_ref, q_ref, coarse_ref, wide_a_ref, wide_b_ref, band1_ref, band2_ref, bias_ref = refs[:8]
    base_ref = refs[8] if keep_base else None
    columns, parts, partial = refs[-3:]
    chip_even = info_ref[1] == 0
    for j in range(4):
        left, right = rows_of(chip_even, wide_a_ref, wide_b_ref, j * 16)
        slab(columns, j * 144, [left, coarse_ref[pl.ds(j * 16, 16), :], right])
    pieces = [columns[pl.ds(j * 144, 144), :] for j in range(4)]
    parts[0], parts[1] = layers(pieces[:3], pieces[1:], band1_ref, band2_ref, bias_ref)

    low = lax.broadcasted_iota(jnp.int32, (8, 128), 0) < 4
    sides = [rows_of(chip_even, wide_a_ref, wide_b_ref, 64 + z * 8) for z in range(0, 8, 2)]
    left, right = zip(*sides)
    for z in range(8):
        for x in range(8):
            here = q_ref[z, x]
            xp = q_ref[z, x + 1] if x < 7 else half_of(right, z)
            xm = q_ref[z, x - 1] if x > 0 else half_of(left, z)
            if z == 0:
                along_z, slope_z = q_ref[1, x], q_ref[1, x]
            elif z == 7:
                along_z, slope_z = q_ref[6, x], -q_ref[6, x]
            else:
                along_z = q_ref[z + 1, x] + q_ref[z - 1, x]
                slope_z = q_ref[z + 1, x] - q_ref[z - 1, x]
            swap = pltpu.roll(here, 4, 0)
            back, ahead = pltpu.roll(swap, 1, 1), pltpu.roll(swap, 127, 1)
            far = jnp.where(low, back, ahead)
            slope_y = jnp.where(low, swap - back, ahead - swap)
            spread = along_z + (xp + xm) + (swap + far)
            u, v, w = (velocity(q_ref, z, x, c, low) for c in range(3))
            advect = u * (xp - xm) + v * slope_y + w * slope_z
            value = (keep_state - 6.0 * step * viscosity) * here
            value = value + (step * viscosity) * spread - (0.5 * step) * advect
            if keep_base:
                value = value + keep_base * base_ref[z, x]
            partial[z, x] = value


def after_body(
    step, info_ref, q_ref, own_columns, own_parts, partial_ref, net_a_ref, net_b_ref,
    band1_ref, band2_ref, bias_ref, div_ref, columns, parts, stress, new_ref,
):
    chip_even, net_even = info_ref[1] == 0, info_ref[2] == 0
    left_at, right_at = jnp.where(chip_even, 160, 112), jnp.where(chip_even, 112, 160)
    for i in range(3):
        starts = [pl.multiple_of(at + i * 16, 16) for at in (left_at, 0, right_at)]
        below, above = zip(*[rows_of(net_even, net_a_ref, net_b_ref, start) for start in starts])
        slab(columns, i * 144, below)
        slab(columns, (3 + i) * 144, above)

    def piece(j):
        if 3 <= j < 7:
            return own_columns[pl.ds((j - 3) * 144, 144), :]
        return columns[pl.ds((j if j < 3 else j - 4) * 144, 144), :]

    for j, k in ((1, 2), (5, 6), (0, 7)):
        parts[j], parts[k] = layers(
            [piece(j + i) for i in range(3)], [piece(k + i) for i in range(3)],
            band1_ref, band2_ref, bias_ref,
        )

    def part(j, at):
        return own_parts[j - 3, at, :] if 3 <= j < 5 else parts[j, at, :]

    for k in range(6):
        rows = []
        for xo in range(6):
            sums = []
            for dy in range(3):
                at = [pl.ds(xo * 72 + (dz * 3 + dy) * 8, 8) for dz in range(3)]
                sums.append(part(k, at[0]) + part(k + 1, at[1]) + part(k + 2, at[2]))
            rows.append(sums[1] + pltpu.roll(sums[0], 1, 1) + pltpu.roll(sums[2], 127, 1))
        stress[pl.ds(k * 48, 48), :] = jnp.concatenate(rows, axis=0).astype(BF16)
    forces = []
    for k in range(1, 5, 2):
        operands = []
        for m in (k, k + 1):
            wide = stress[pl.ds(m * 48, 48), :].astype(F32)
            operands.append(
                jnp.concatenate(
                    [
                        stress[pl.ds((m - 1) * 48, 144), :],
                        pltpu.roll(wide, 1, 1).astype(BF16),
                        pltpu.roll(wide, 127, 1).astype(BF16),
                    ],
                    axis=0,
                )
            )
        both = step * jnp.dot(
            div_ref[...], jnp.concatenate(operands, axis=1), preferred_element_type=F32
        )
        forces += [both[:, :128], both[:, 128:]]

    low = lax.broadcasted_iota(jnp.int32, (8, 128), 0) < 4
    ends = [rows_of(net_even, net_a_ref, net_b_ref, 48 + x * 8) for x in range(0, 8, 2)]
    below, above = zip(*ends)
    for z in range(8):
        for x in range(8):
            value = partial_ref[z, x] + forces[z // 2][(x // 2) * 8 : (x // 2) * 8 + 8]
            if z == 0:
                w = velocity(q_ref, z, x, 2, low)
                value = value + (step * viscosity + (0.5 * step) * w) * half_of(below, x)
            if z == 7:
                w = velocity(q_ref, z, x, 2, low)
                value = value + (step * viscosity - (0.5 * step) * w) * half_of(above, x)
            new_ref[z, x] = value


def after_kernel(step, *refs):
    ins, outs, scratch = refs[:11], refs[11:16], refs[16:]
    after_body(step, *ins, *scratch, outs[0])
    emit_messages(ins[0], *outs)


def last_kernel(step, *refs):
    ins, outs, scratch, new = refs[:11], refs[11:13], refs[13:-1], refs[-1]
    core = ins[0][0]
    after_body(step, *ins, *scratch, new)
    outs[0][...] = new[:, pl.ds(core * 4, 4)].reshape(256, 128)
    outs[1][...] = new[:, pl.ds((1 - core) * 4, 4)].reshape(256, 128)


def finish_kernel(info_ref, own_ref, other_ref, parity_ref, out_ref, native, flat):
    core = info_ref[0]
    lane = lanes_of((256, 128))
    low = jnp.where(core == 0, own_ref[...], other_ref[...])
    high = jnp.where(core == 0, other_ref[...], own_ref[...])
    native[...] = jnp.where(
        lane < HALF, pltpu.roll(low, 128 - EDGE, 1), pltpu.roll(high, HALF - EDGE, 1)
    )
    halves = [
        jnp.concatenate([native[pl.ds(p * 4 + c, 32, stride=8), :] for c in range(4)], axis=0)
        for p in range(2)
    ]
    split = lax.dot_general(
        thirds(jnp.concatenate(halves, axis=1)),
        parity_ref[...],
        (((1,), (1,)), ((), ())),
        preferred_element_type=F32,
    )
    flat[...] = split[:128] + split[128:256] + split[256:]
    for c in range(4):
        for z in range(8):
            out_ref[c, z] = flat[pl.ds((c * 8 + z) * 4, 4), :]


def chip_swap(value, odd):
    size = lax.axis_size("wide")
    pairs = []
    for i in range(size):
        chip, core = divmod(i, 2)
        to = chip + 1 if (chip + odd) % 2 == 0 else chip - 1
        pairs.append((i, (2 * to + core) % size))
    return lax.ppermute(value, "wide", pairs)


def net_swap(value, odd):
    size = lax.axis_size("net")
    pairs = [(i, (i + 1 if (i + odd) % 2 == 0 else i - 1) % size) for i in range(size)]
    return lax.ppermute(value, "net", pairs)


def partner(value):
    return lax.ppermute(value, "wide", [(i, i ^ 1) for i in range(lax.axis_size("wide"))])


def edge_shift(value, cross):
    wide, narrow = lax.axis_size("wide"), lax.axis_size("narrow")
    pairs = []
    for w in range(wide):
        for r in range(narrow):
            if cross:
                step, to = (-1 if w % 2 == 0 else 1), w ^ 1
            else:
                step, to = (1 if w % 2 == 0 else -1), w
            pairs.append((w * narrow + r, to * narrow + (r + step) % narrow))
    return lax.ppermute(value, ("wide", "narrow"), pairs)


def per_device(fields, conv1_weight, conv1_bias, conv2_weight):
    wide, net = lax.axis_index("wide"), lax.axis_index("net")
    info = jnp.stack([wide % 2, (wide // 2) % 2, net % 2]).astype(jnp.int32)
    native, same, cross, parity = call(
        pack_kernel,
        [((256, 128), F32), ((32, 128), F32), ((32, 128), F32), ((256, 256), BF16)],
        [pltpu.VMEM((128, 256), F32)],
        info, fields,
    )
    other = near(partner(native))
    same = near(edge_shift(same, False))
    cross = near(edge_shift(cross, True))
    fixed = call(
        weights_kernel,
        [((256, 512), BF16), ((432, 256), BF16), ((32, 128), F32)],
        [pltpu.VMEM((32, 512), F32), pltpu.VMEM((72, 256), F32), pltpu.VMEM((432, 256), F32)],
        info, conv1_weight, conv2_weight, conv1_bias.reshape(1, 32),
    )
    fixed = (*map(near, fixed), near(jnp.asarray(divergence_matrix(), BF16)))
    base, *messages = call(
        assemble_kernel,
        [((8, 8, 8, 128), F32)] + MESSAGES,
        [],
        info, near(native), other, same, cross, fixed[2],
    )
    state = base = near(base)
    even = net % 2 == 0
    stages = ((0.0, 1.0, time_step), (0.75, 0.25, 0.25 * time_step), (1.0 / 3.0, 2.0 / 3.0, 2.0 / 3.0 * time_step))
    scratch = [
        pltpu.VMEM((864, 128), BF16),
        pltpu.VMEM((8, 432, 128), F32),
        pltpu.VMEM((288, 128), BF16),
    ]
    for stage, weights in enumerate(stages):
        wide_a, wide_b, net_a, net_b = messages
        got_a, got_b = chip_swap(wide_a, 0), chip_swap(wide_b, 1)
        rows_a = [jnp.where(even, got[16:64], got[:48]) for got in (got_a, got_b)]
        rows_b = [jnp.where(even, got[:48], got[16:64]) for got in (got_a, got_b)]
        far_a = net_swap(jnp.concatenate([net_a, *rows_a], axis=0), 0)
        far_b = net_swap(jnp.concatenate([net_b, *rows_b], axis=0), 1)
        before = call(
            functools.partial(before_kernel, weights),
            [((576, 128), BF16), ((2, 432, 128), F32), ((8, 8, 8, 128), F32)],
            [],
            info, state, *map(near, (wide_a, got_a, got_b)), *fixed[:3], *([base] if stage else []),
        )
        ins = (info, state, *map(near, before), near(far_a), near(far_b), *fixed)
        if stage < 2:
            state, *messages = call(
                functools.partial(after_kernel, weights[2]),
                [((8, 8, 8, 128), F32)] + MESSAGES,
                scratch,
                *ins,
            )
            state = near(state)
    own, away = call(
        functools.partial(last_kernel, stages[2][2]),
        [((256, 128), F32)] * 2,
        scratch + [pltpu.VMEM((8, 8, 8, 128), F32)],
        *ins,
    )
    return call(
        finish_kernel,
        None,
        [pltpu.VMEM((256, 128), F32), pltpu.VMEM((128, 256), F32)],
        info, near(own), near(partner(away)), near(parity),
        result=jax.ShapeDtypeStruct(fields.shape, F32),
    )


def solution(mesh):
    in_specs = (P(None, "net", "wide", "narrow"), P(), P(), P())
    out_specs = P(None, "net", "wide", "narrow")
    return jax.shard_map(
        per_device, mesh=mesh, in_specs=in_specs, out_specs=out_specs, check_vma=False
    )
```

```python
import functools

import jax
import jax.numpy as jnp
import numpy as np
from jax import lax
from jax.experimental import pallas as pl
from jax.experimental.pallas import tpu as pltpu
from jax.sharding import PartitionSpec as P

time_step = 0.2
viscosity = 0.05
EDGE = 9
HALF = 64
VMEM_LIMIT = 16 << 20
F32 = jnp.float32
BF16 = jnp.bfloat16
VM = pl.BlockSpec(memory_space=pltpu.VMEM)
SM = pl.BlockSpec(memory_space=pltpu.SMEM)


def divergence_matrix():
    m = np.zeros((4, 2, 4, 5, 6, 8), np.float32)
    sx, sy, sz = (0, 3, 4), (3, 1, 5), (4, 5, 2)
    for x in range(4):
        for comp in range(3):
            m[x, :, comp, 1, x + 2, sx[comp]] += 0.25
            m[x, :, comp, 1, x, sx[comp]] -= 0.25
            m[x, :, comp, 4, x + 1, sy[comp]] += 0.25
            m[x, :, comp, 3, x + 1, sy[comp]] -= 0.25
            m[x, :, comp, 2, x + 1, sz[comp]] += 0.25
            m[x, :, comp, 0, x + 1, sz[comp]] -= 0.25
    return m.reshape(32, 240)


def near(value):
    return pltpu.with_memory_space_constraint(value, pltpu.VMEM)


def call(kernel, outs, scratch, info, *args, result=None):
    return pl.pallas_call(
        kernel,
        out_shape=result or [pltpu.VMEM(s, d) for s, d in outs],
        in_specs=[SM] + [VM] * len(args),
        out_specs=VM if result else [VM] * len(outs),
        scratch_shapes=scratch,
        compiler_params=pltpu.CompilerParams(vmem_limit_bytes=VMEM_LIMIT),
    )(info, *args)


def lanes_of(shape):
    return lax.broadcasted_iota(jnp.int32, shape, len(shape) - 1)


def thirds(value):
    first = value.astype(BF16)
    rest = value - first.astype(F32)
    second = rest.astype(BF16)
    third = (rest - second.astype(F32)).astype(BF16)
    return jnp.concatenate([first, second, third], axis=0)


def pack_kernel(info_ref, fields_ref, native_ref, same_ref, cross_ref, parity_ref, flat):
    core = info_ref[0]
    row, col = lax.broadcasted_iota(jnp.int32, (256, 256), 0), lanes_of((256, 256))
    source = jnp.where(col < 128, 2 * col, 2 * col - 255)
    parity_ref[...] = jnp.where(row == source, 1.0, 0.0).astype(F32).astype(BF16)
    for c in range(4):
        for z in range(8):
            flat[pl.ds((c * 8 + z) * 4, 4), :] = fields_ref[c, z]
    split = jnp.dot(thirds(flat[...]), parity_ref[...], preferred_element_type=F32)
    parts = split[:128] + split[128:256] + split[256:]
    for p in range(2):
        for c in range(4):
            native_ref[pl.ds(p * 4 + c, 32, stride=8), :] = parts[
                c * 32 : (c + 1) * 32, p * 128 : (p + 1) * 128
            ]
    lane = lanes_of((32, 128))
    for out_ref, take_last in ((same_ref, core == 0), (cross_ref, core == 1)):
        offset = jnp.where(take_last, EDGE, 0)
        total = jnp.zeros((32, 128), F32)
        for g in range(8):
            moved = pltpu.roll(native_ref[pl.ds(g * 32, 32), :], g * 16 + offset, 1)
            total = jnp.where((lane >= g * 16) & (lane < g * 16 + EDGE), moved, total)
        out_ref[...] = total


def emit_messages(info_ref, q_ref, wide_a_ref, wide_b_ref, net_a_ref, net_b_ref):
    chip_even, net_even = info_ref[1] == 0, info_ref[2] == 0
    low = lax.broadcasted_iota(jnp.int32, (8, 128), 0) < 4
    slabs = []
    for zc in range(4):
        means = []
        for xc in range(4):
            t = (q_ref[2 * zc, 2 * xc] + q_ref[2 * zc, 2 * xc + 1]) + (
                q_ref[2 * zc + 1, 2 * xc] + q_ref[2 * zc + 1, 2 * xc + 1]
            )
            means.append((t + pltpu.roll(t, 4, 0)) * 0.125)
        slab = jnp.concatenate(
            [jnp.where(low, means[0], means[1]), jnp.where(low, means[2], means[3])], axis=0
        )
        slabs.append(slab)
        wide_a_ref[pl.ds(zc * 16, 16), :] = slab.astype(BF16)
        wide_b_ref[pl.ds(zc * 16, 16), :] = slab.astype(BF16)
    for zc in range(3):
        at = pl.ds(zc * 16, 16)
        net_a_ref[at, :] = jnp.where(net_even, slabs[zc + 1], slabs[zc]).astype(BF16)
        net_b_ref[at, :] = jnp.where(net_even, slabs[zc], slabs[zc + 1]).astype(BF16)
    xa, xb = jnp.where(chip_even, 7, 0), jnp.where(chip_even, 0, 7)
    za, zb = jnp.where(net_even, 7, 0), jnp.where(net_even, 0, 7)
    for z in range(0, 8, 2):
        at = pl.ds(64 + z * 8, 16)
        wide_a_ref[at, :] = jnp.concatenate([q_ref[z, xa], q_ref[z + 1, xa]], axis=0).astype(BF16)
        wide_b_ref[at, :] = jnp.concatenate([q_ref[z, xb], q_ref[z + 1, xb]], axis=0).astype(BF16)
    for x in range(0, 8, 2):
        at = pl.ds(48 + x * 8, 16)
        net_a_ref[at, :] = jnp.concatenate([q_ref[za, x], q_ref[za, x + 1]], axis=0).astype(BF16)
        net_b_ref[at, :] = jnp.concatenate([q_ref[zb, x], q_ref[zb, x + 1]], axis=0).astype(BF16)


MESSAGES = [((128, 128), BF16), ((128, 128), BF16), ((112, 128), BF16), ((112, 128), BF16)]


def assemble_kernel(
    info_ref, own_ref, other_ref, same_ref, cross_ref, ready_ref,
    q_ref, wide_a_ref, wide_b_ref, net_a_ref, net_b_ref,
):
    core = info_ref[0]
    lane = lanes_of((32, 128))
    begin = jnp.where(core == 0, EDGE, 0)
    inside = (lane >= begin) & (lane < begin + HALF + EDGE)
    shift = jnp.where(core == 0, EDGE, HALF + EDGE)
    start = jnp.where(core == 0, 128, HALF + EDGE + 128)
    for block_ref, edge_ref, position in ((own_ref, same_ref, core), (other_ref, cross_ref, 1 - core)):
        edge = edge_ref[...]
        for g in range(8):
            block = pltpu.roll(block_ref[pl.ds(g * 32, 32), :], shift, 1)
            block = jnp.where(inside, block, pltpu.roll(edge, lax.rem(start - g * 16, 128), 1))
            q_ref[g, pl.ds(position * 4, 4)] = block.reshape(4, 8, 128)
    emit_messages(info_ref, q_ref, wide_a_ref, wide_b_ref, net_a_ref, net_b_ref)


def weights_kernel(info_ref, w1_ref, w2_ref, b_ref, band1_ref, band2_ref, flat1, flat2, tall):
    flat1[...] = jnp.zeros_like(flat1)
    flat2[...] = jnp.zeros_like(flat2)
    for dz in range(3):
        for dx in range(3):
            for dy in range(3):
                tap = 9 * dz + 3 * dx + dy
                flat1[:, pl.ds((dz * 3 + dy) * 48 + (1 + dx) * 4, 4)] = w1_ref[tap].astype(F32)
                flat2[pl.ds((dz * 3 + dy) * 8, 6), pl.ds(dx * 32, 32)] = w2_ref[tap].astype(F32)
    square = jnp.broadcast_to(b_ref[...], (32, 32))
    diagonal = lanes_of((32, 32)) == lax.broadcasted_iota(jnp.int32, (32, 32), 0)
    bias = 0.5 * jnp.sum(jnp.where(diagonal, square, 0.0), axis=1, keepdims=True)
    first = bias.astype(BF16).astype(F32)
    second = (bias - first).astype(BF16).astype(F32)
    lane = lanes_of((32, 128))
    extra = jnp.where(lane == 48, first, jnp.where(lane == 49, second, bias - first - second))
    for xo in range(8):
        moved = 0.5 * pltpu.roll(flat1[...], 4 * xo, 1)
        end = jnp.where((lane >= 48) & (lane < 51), extra, moved[:, 384:])
        band1_ref[pl.ds(xo * 32, 32), pl.ds(0, 384)] = moved[:, :384].astype(BF16)
        band1_ref[pl.ds(xo * 32, 32), pl.ds(384, 128)] = end.astype(BF16)
    for xo in range(6):
        for dz in range(3):
            tall[pl.ds(xo * 24, 24), pl.ds(dz * 256, 256)] = pltpu.roll(
                flat2[pl.ds(dz * 24, 24), :], 32 * xo, 1
            )
    band2_ref[...] = tall[...].astype(BF16)


def slab(ref, start, pieces):
    for i, piece in enumerate(pieces):
        wide = piece.astype(F32)
        ref[pl.ds(start + i * 16, 16), :] = pltpu.roll(wide, 1, 1).astype(BF16)
        ref[pl.ds(start + 48 + i * 16, 16), :] = wide.astype(BF16)
        ref[pl.ds(start + 96 + i * 16, 16), :] = pltpu.roll(wide, 127, 1).astype(BF16)


def rows_of(even, a_ref, b_ref, start):
    a = a_ref[pl.ds(start, 16), :].astype(F32)
    b = b_ref[pl.ds(start, 16), :].astype(F32)
    return jnp.where(even, b, a), jnp.where(even, a, b)


def first_layer(first, second, band1_ref, pre_ref):
    ones = jnp.where(lax.broadcasted_iota(jnp.int32, (16, 256), 0) < 3, 1.0, 0.0).astype(BF16)
    rows = jnp.concatenate(
        [jnp.concatenate(first, axis=0), jnp.concatenate(second, axis=0)], axis=1
    )
    rows = jnp.concatenate([rows, ones], axis=0)
    pre_ref[...] = jnp.dot(band1_ref[:, :448], rows, preferred_element_type=F32)


def activate(pre_ref, hidden_ref):
    scale = 2.0 * 0.7978845608028654
    for xo in range(8):
        at = pl.ds(xo * 32, 32)
        half = pre_ref[at, :]
        inner = half * (scale + (4.0 * 0.044715 * scale) * (half * half))
        hidden_ref[at, :] = (half + half * jnp.tanh(inner)).astype(BF16)


def half_of(pair, i):
    return pair[i // 2][(i % 2) * 8 : (i % 2) * 8 + 8]


def velocity(q_ref, z, x, c, low):
    first = jnp.broadcast_to(q_ref[z, x, c : c + 1, :], (8, 128))
    second = jnp.broadcast_to(q_ref[z, x, c + 4 : c + 5, :], (8, 128))
    return jnp.where(low, first, second)


def before_kernel(weights, *refs):
    keep_base, keep_state, step = weights
    info_ref, q_ref, coarse_ref, wide_a_ref, wide_b_ref, band1_ref = refs[:6]
    base_ref = refs[6] if keep_base else None
    columns, hidden, partial, pre = refs[-4:]
    chip_even = info_ref[1] == 0
    for j in range(4):
        left, right = rows_of(chip_even, wide_a_ref, wide_b_ref, j * 16)
        slab(columns, j * 144, [left, coarse_ref[pl.ds(j * 16, 16), :], right])
    pieces = [columns[pl.ds(j * 144, 144), :] for j in range(4)]
    first_layer(pieces[:3], pieces[1:], band1_ref, pre)
    activate(pre, hidden)

    low = lax.broadcasted_iota(jnp.int32, (8, 128), 0) < 4
    sides = [rows_of(chip_even, wide_a_ref, wide_b_ref, 64 + z * 8) for z in range(0, 8, 2)]
    left, right = zip(*sides)
    for z in range(8):
        for x in range(8):
            here = q_ref[z, x]
            xp = q_ref[z, x + 1] if x < 7 else half_of(right, z)
            xm = q_ref[z, x - 1] if x > 0 else half_of(left, z)
            if z == 0:
                along_z, slope_z = q_ref[1, x], q_ref[1, x]
            elif z == 7:
                along_z, slope_z = q_ref[6, x], -q_ref[6, x]
            else:
                along_z = q_ref[z + 1, x] + q_ref[z - 1, x]
                slope_z = q_ref[z + 1, x] - q_ref[z - 1, x]
            swap = pltpu.roll(here, 4, 0)
            back, ahead = pltpu.roll(swap, 1, 1), pltpu.roll(swap, 127, 1)
            far = jnp.where(low, back, ahead)
            slope_y = jnp.where(low, swap - back, ahead - swap)
            spread = along_z + (xp + xm) + (swap + far)
            u, v, w = (velocity(q_ref, z, x, c, low) for c in range(3))
            advect = u * (xp - xm) + v * slope_y + w * slope_z
            value = (keep_state - 6.0 * step * viscosity) * here
            value = value + (step * viscosity) * spread - (0.5 * step) * advect
            if keep_base:
                value = value + keep_base * base_ref[z, x]
            partial[z, x] = value


def after_body(
    step, info_ref, q_ref, own_columns, own_hidden, partial_ref, net_a_ref, net_b_ref,
    band1_ref, band2_ref, div_ref, columns, stress, pre, hidden, new_ref,
):
    chip_even, net_even = info_ref[1] == 0, info_ref[2] == 0
    left_at, right_at = jnp.where(chip_even, 160, 112), jnp.where(chip_even, 112, 160)
    for i in range(3):
        starts = [pl.multiple_of(at + i * 16, 16) for at in (left_at, 0, right_at)]
        below, above = zip(*[rows_of(net_even, net_a_ref, net_b_ref, start) for start in starts])
        slab(columns, i * 144, below)
        slab(columns, (3 + i) * 144, above)

    def piece(j):
        if 3 <= j < 7:
            return own_columns[pl.ds((j - 3) * 144, 144), :]
        return columns[pl.ds((j if j < 3 else j - 4) * 144, 144), :]

    pairs = ((1, 2), (5, 6), (0, 7))

    def conv1(i):
        first, second = ([piece(j + dz) for dz in range(3)] for j in pairs[i])
        first_layer(first, second, band1_ref, pre.at[i])

    def gelu(i):
        activate(pre.at[i], hidden.at[i])

    def hidden_of(j):
        if 3 <= j < 5:
            return own_hidden[:, pl.ds((j - 3) * 128, 128)]
        i = (2, 0, 0, None, None, 1, 1, 2)[j]
        return hidden[i, :, pl.ds(pairs[i].index(j) * 128, 128)]

    def levels(k, m):
        rows = jnp.concatenate(
            [
                jnp.concatenate([hidden_of(n + dz) for dz in range(3)], axis=0)
                for n in (k, m)
            ],
            axis=1,
        )
        both = jnp.dot(band2_ref[...], rows, preferred_element_type=F32)
        for n, sums in ((k, both[:, :128]), (m, both[:, 128:])):
            tiles = []
            for xo in range(6):
                at = xo * 24
                tiles.append(
                    sums[at + 8 : at + 16]
                    + pltpu.roll(sums[at : at + 8], 1, 1)
                    + pltpu.roll(sums[at + 16 : at + 24], 127, 1)
                )
            stress[pl.ds(n * 48, 48), :] = jnp.concatenate(tiles, axis=0).astype(BF16)

    low = lax.broadcasted_iota(jnp.int32, (8, 128), 0) < 4
    ends = [rows_of(net_even, net_a_ref, net_b_ref, 48 + x * 8) for x in range(0, 8, 2)]
    below, above = zip(*ends)

    def advance(k, m):
        operands = []
        for n in (k, m):
            wide = stress[pl.ds(n * 48, 48), :].astype(F32)
            operands.append(
                jnp.concatenate(
                    [
                        stress[pl.ds((n - 1) * 48, 144), :],
                        pltpu.roll(wide, 1, 1).astype(BF16),
                        pltpu.roll(wide, 127, 1).astype(BF16),
                    ],
                    axis=0,
                )
            )
        both = step * jnp.dot(
            div_ref[...], jnp.concatenate(operands, axis=1), preferred_element_type=F32
        )
        for n, force in ((k, both[:, :128]), (m, both[:, 128:])):
            for z in (2 * n - 2, 2 * n - 1):
                for x in range(8):
                    value = partial_ref[z, x] + force[(x // 2) * 8 : (x // 2) * 8 + 8]
                    if z == 0:
                        w = velocity(q_ref, z, x, 2, low)
                        factor = step * viscosity + (0.5 * step) * w
                        value = value + factor * half_of(below, x)
                    if z == 7:
                        w = velocity(q_ref, z, x, 2, low)
                        factor = step * viscosity - (0.5 * step) * w
                        value = value + factor * half_of(above, x)
                    new_ref[z, x] = value

    conv1(0)
    conv1(1)
    gelu(0)
    conv1(2)
    gelu(1)
    levels(1, 2)
    gelu(2)
    levels(3, 4)
    levels(0, 5)
    advance(2, 3)
    advance(1, 4)


def after_kernel(step, *refs):
    ins, outs, scratch = refs[:10], refs[10:15], refs[15:]
    after_body(step, *ins, *scratch, outs[0])
    emit_messages(ins[0], *outs)


def last_kernel(step, *refs):
    ins, outs, scratch, new = refs[:10], refs[10:12], refs[12:-1], refs[-1]
    core = ins[0][0]
    after_body(step, *ins, *scratch, new)
    outs[0][...] = new[:, pl.ds(core * 4, 4)].reshape(256, 128)
    outs[1][...] = new[:, pl.ds((1 - core) * 4, 4)].reshape(256, 128)


def finish_kernel(info_ref, own_ref, other_ref, parity_ref, out_ref, native, flat):
    core = info_ref[0]
    lane = lanes_of((256, 128))
    low = jnp.where(core == 0, own_ref[...], other_ref[...])
    high = jnp.where(core == 0, other_ref[...], own_ref[...])
    native[...] = jnp.where(
        lane < HALF, pltpu.roll(low, 128 - EDGE, 1), pltpu.roll(high, HALF - EDGE, 1)
    )
    halves = [
        jnp.concatenate([native[pl.ds(p * 4 + c, 32, stride=8), :] for c in range(4)], axis=0)
        for p in range(2)
    ]
    split = lax.dot_general(
        thirds(jnp.concatenate(halves, axis=1)),
        parity_ref[...],
        (((1,), (1,)), ((), ())),
        preferred_element_type=F32,
    )
    flat[...] = split[:128] + split[128:256] + split[256:]
    for c in range(4):
        for z in range(8):
            out_ref[c, z] = flat[pl.ds((c * 8 + z) * 4, 4), :]


def chip_swap(value, odd):
    size = lax.axis_size("wide")
    pairs = []
    for i in range(size):
        chip, core = divmod(i, 2)
        to = chip + 1 if (chip + odd) % 2 == 0 else chip - 1
        pairs.append((i, (2 * to + core) % size))
    return lax.ppermute(value, "wide", pairs)


def net_swap(value, odd):
    size = lax.axis_size("net")
    pairs = [(i, (i + 1 if (i + odd) % 2 == 0 else i - 1) % size) for i in range(size)]
    return lax.ppermute(value, "net", pairs)


def partner(value):
    return lax.ppermute(value, "wide", [(i, i ^ 1) for i in range(lax.axis_size("wide"))])


def edge_shift(value, cross):
    wide, narrow = lax.axis_size("wide"), lax.axis_size("narrow")
    pairs = []
    for w in range(wide):
        for r in range(narrow):
            if cross:
                step, to = (-1 if w % 2 == 0 else 1), w ^ 1
            else:
                step, to = (1 if w % 2 == 0 else -1), w
            pairs.append((w * narrow + r, to * narrow + (r + step) % narrow))
    return lax.ppermute(value, ("wide", "narrow"), pairs)


def per_device(fields, conv1_weight, conv1_bias, conv2_weight):
    wide, net = lax.axis_index("wide"), lax.axis_index("net")
    info = jnp.stack([wide % 2, (wide // 2) % 2, net % 2]).astype(jnp.int32)
    native, same, cross, parity = call(
        pack_kernel,
        [((256, 128), F32), ((32, 128), F32), ((32, 128), F32), ((256, 256), BF16)],
        [pltpu.VMEM((128, 256), F32)],
        info, fields,
    )
    other = near(partner(native))
    same = near(edge_shift(same, False))
    cross = near(edge_shift(cross, True))
    fixed = call(
        weights_kernel,
        [((256, 512), BF16), ((144, 768), BF16)],
        [pltpu.VMEM((32, 512), F32), pltpu.VMEM((72, 256), F32), pltpu.VMEM((144, 768), F32)],
        info, conv1_weight, conv2_weight, conv1_bias.reshape(1, 32),
    )
    fixed = (*map(near, fixed), near(jnp.asarray(divergence_matrix(), BF16)))
    base, *messages = call(
        assemble_kernel,
        [((8, 8, 8, 128), F32)] + MESSAGES,
        [],
        info, near(native), other, same, cross, fixed[1],
    )
    state = base = near(base)
    even = net % 2 == 0
    stages = ((0.0, 1.0, time_step), (0.75, 0.25, 0.25 * time_step), (1.0 / 3.0, 2.0 / 3.0, 2.0 / 3.0 * time_step))
    scratch = [
        pltpu.VMEM((864, 128), BF16),
        pltpu.VMEM((288, 128), BF16),
        pltpu.VMEM((3, 256, 256), F32),
        pltpu.VMEM((3, 256, 256), BF16),
    ]
    for stage, weights in enumerate(stages):
        wide_a, wide_b, net_a, net_b = messages
        got_a, got_b = chip_swap(wide_a, 0), chip_swap(wide_b, 1)
        rows_a = [jnp.where(even, got[16:64], got[:48]) for got in (got_a, got_b)]
        rows_b = [jnp.where(even, got[:48], got[16:64]) for got in (got_a, got_b)]
        far_a = net_swap(jnp.concatenate([net_a, *rows_a], axis=0), 0)
        far_b = net_swap(jnp.concatenate([net_b, *rows_b], axis=0), 1)
        before = call(
            functools.partial(before_kernel, weights),
            [((576, 128), BF16), ((256, 256), BF16), ((8, 8, 8, 128), F32)],
            [pltpu.VMEM((256, 256), F32)],
            info, state, *map(near, (wide_a, got_a, got_b)), fixed[0], *([base] if stage else []),
        )
        ins = (info, state, *map(near, before), near(far_a), near(far_b), *fixed)
        if stage < 2:
            state, *messages = call(
                functools.partial(after_kernel, weights[2]),
                [((8, 8, 8, 128), F32)] + MESSAGES,
                scratch,
                *ins,
            )
            state = near(state)
    own, away = call(
        functools.partial(last_kernel, stages[2][2]),
        [((256, 128), F32)] * 2,
        scratch + [pltpu.VMEM((8, 8, 8, 128), F32)],
        *ins,
    )
    return call(
        finish_kernel,
        None,
        [pltpu.VMEM((256, 128), F32), pltpu.VMEM((128, 256), F32)],
        info, near(own), near(partner(away)), near(parity),
        result=jax.ShapeDtypeStruct(fields.shape, F32),
    )


def solution(mesh):
    in_specs = (P(None, "net", "wide", "narrow"), P(), P(), P())
    out_specs = P(None, "net", "wide", "narrow")
    return jax.shard_map(
        per_device, mesh=mesh, in_specs=in_specs, out_specs=out_specs, check_vma=False
    )
```

```python
import functools

import jax
import jax.numpy as jnp
import numpy as np
from jax import lax
from jax.experimental import pallas as pl
from jax.experimental.pallas import tpu as pltpu
from jax.sharding import PartitionSpec as P

time_step = 0.2
viscosity = 0.05
EDGE = 9
HALF = 64
VMEM_LIMIT = 16 << 20
F32 = jnp.float32
BF16 = jnp.bfloat16
VM = pl.BlockSpec(memory_space=pltpu.VMEM)
SM = pl.BlockSpec(memory_space=pltpu.SMEM)


def divergence_matrix():
    m = np.zeros((4, 2, 4, 5, 6, 8), np.float32)
    sx, sy, sz = (0, 3, 4), (3, 1, 5), (4, 5, 2)
    for x in range(4):
        for comp in range(3):
            m[x, :, comp, 1, x + 2, sx[comp]] += 0.25
            m[x, :, comp, 1, x, sx[comp]] -= 0.25
            m[x, :, comp, 4, x + 1, sy[comp]] += 0.25
            m[x, :, comp, 3, x + 1, sy[comp]] -= 0.25
            m[x, :, comp, 2, x + 1, sz[comp]] += 0.25
            m[x, :, comp, 0, x + 1, sz[comp]] -= 0.25
    return m.reshape(32, 240)


def near(value):
    return pltpu.with_memory_space_constraint(value, pltpu.VMEM)


def call(kernel, outs, scratch, info, *args, result=None):
    return pl.pallas_call(
        kernel,
        out_shape=result or [pltpu.VMEM(s, d) for s, d in outs],
        in_specs=[SM] + [VM] * len(args),
        out_specs=VM if result else [VM] * len(outs),
        scratch_shapes=scratch,
        compiler_params=pltpu.CompilerParams(vmem_limit_bytes=VMEM_LIMIT),
    )(info, *args)


def lanes_of(shape):
    return lax.broadcasted_iota(jnp.int32, shape, len(shape) - 1)


def thirds(value):
    first = value.astype(BF16)
    rest = value - first.astype(F32)
    second = rest.astype(BF16)
    third = (rest - second.astype(F32)).astype(BF16)
    return jnp.concatenate([first, second, third], axis=0)


def pack_kernel(info_ref, fields_ref, native_ref, same_ref, cross_ref, parity_ref, flat):
    core = info_ref[0]
    row, col = lax.broadcasted_iota(jnp.int32, (256, 256), 0), lanes_of((256, 256))
    source = jnp.where(col < 128, 2 * col, 2 * col - 255)
    parity_ref[...] = jnp.where(row == source, 1.0, 0.0).astype(F32).astype(BF16)
    for c in range(4):
        for z in range(8):
            flat[pl.ds((c * 8 + z) * 4, 4), :] = fields_ref[c, z]
    split = jnp.dot(thirds(flat[...]), parity_ref[...], preferred_element_type=F32)
    parts = split[:128] + split[128:256] + split[256:]
    for p in range(2):
        for c in range(4):
            native_ref[pl.ds(p * 4 + c, 32, stride=8), :] = parts[
                c * 32 : (c + 1) * 32, p * 128 : (p + 1) * 128
            ]
    lane = lanes_of((32, 128))
    for out_ref, take_last in ((same_ref, core == 0), (cross_ref, core == 1)):
        offset = jnp.where(take_last, EDGE, 0)
        total = jnp.zeros((32, 128), F32)
        for g in range(8):
            moved = pltpu.roll(native_ref[pl.ds(g * 32, 32), :], g * 16 + offset, 1)
            total = jnp.where((lane >= g * 16) & (lane < g * 16 + EDGE), moved, total)
        out_ref[...] = total


def emit_messages(info_ref, q_ref, wide_a_ref, wide_b_ref, net_a_ref, net_b_ref):
    chip_even = info_ref[1] == 0
    low = lax.broadcasted_iota(jnp.int32, (8, 128), 0) < 4
    slabs = []
    for zc in range(4):
        means = []
        for xc in range(4):
            t = (q_ref[2 * zc, 2 * xc] + q_ref[2 * zc, 2 * xc + 1]) + (
                q_ref[2 * zc + 1, 2 * xc] + q_ref[2 * zc + 1, 2 * xc + 1]
            )
            means.append((t + pltpu.roll(t, 4, 0)) * 0.125)
        slab = jnp.concatenate(
            [jnp.where(low, means[0], means[1]), jnp.where(low, means[2], means[3])], axis=0
        )
        slabs.append(slab)
        wide_a_ref[pl.ds(zc * 16, 16), :] = slab.astype(BF16)
        wide_b_ref[pl.ds(zc * 16, 16), :] = slab.astype(BF16)
    for zc in range(3):
        at = pl.ds(zc * 16, 16)
        net_a_ref[at, :] = slabs[zc + 1].astype(BF16)
        net_b_ref[at, :] = slabs[zc].astype(BF16)
    xa, xb = jnp.where(chip_even, 7, 0), jnp.where(chip_even, 0, 7)
    for z in range(0, 8, 2):
        at = pl.ds(64 + z * 8, 16)
        wide_a_ref[at, :] = jnp.concatenate([q_ref[z, xa], q_ref[z + 1, xa]], axis=0).astype(BF16)
        wide_b_ref[at, :] = jnp.concatenate([q_ref[z, xb], q_ref[z + 1, xb]], axis=0).astype(BF16)
    for x in range(0, 8, 2):
        at = pl.ds(48 + x * 8, 16)
        net_a_ref[at, :] = jnp.concatenate([q_ref[7, x], q_ref[7, x + 1]], axis=0).astype(BF16)
        net_b_ref[at, :] = jnp.concatenate([q_ref[0, x], q_ref[0, x + 1]], axis=0).astype(BF16)


MESSAGES = [((128, 128), BF16), ((128, 128), BF16), ((112, 128), BF16), ((112, 128), BF16)]


def assemble_kernel(
    info_ref, own_ref, other_ref, same_ref, cross_ref, ready_ref,
    q_ref, wide_a_ref, wide_b_ref, net_a_ref, net_b_ref,
):
    core = info_ref[0]
    lane = lanes_of((32, 128))
    begin = jnp.where(core == 0, EDGE, 0)
    inside = (lane >= begin) & (lane < begin + HALF + EDGE)
    shift = jnp.where(core == 0, EDGE, HALF + EDGE)
    start = jnp.where(core == 0, 128, HALF + EDGE + 128)
    for block_ref, edge_ref, position in ((own_ref, same_ref, core), (other_ref, cross_ref, 1 - core)):
        edge = edge_ref[...]
        for g in range(8):
            block = pltpu.roll(block_ref[pl.ds(g * 32, 32), :], shift, 1)
            block = jnp.where(inside, block, pltpu.roll(edge, lax.rem(start - g * 16, 128), 1))
            q_ref[jnp.where(info_ref[2] == 0, g, 7 - g), pl.ds(position * 4, 4)] = block.reshape(4, 8, 128)
    emit_messages(info_ref, q_ref, wide_a_ref, wide_b_ref, net_a_ref, net_b_ref)


def weights_kernel(
    info_ref, w1_ref, w2_ref, b_ref, div_ref, band1_ref, band2_ref, signed_ref, flat1, flat2, tall
):
    flat1[...] = jnp.zeros_like(flat1)
    flat2[...] = jnp.zeros_like(flat2)
    for dz in range(3):
        for dx in range(3):
            for dy in range(3):
                tap = 9 * jnp.where(info_ref[2] == 0, dz, 2 - dz) + 3 * dx + dy
                flat1[:, pl.ds((dz * 3 + dy) * 48 + (1 + dx) * 4, 4)] = w1_ref[tap].astype(F32)
                flat2[pl.ds((dz * 3 + dy) * 8, 6), pl.ds(dx * 32, 32)] = w2_ref[tap].astype(F32)
    square = jnp.broadcast_to(b_ref[...], (32, 32))
    diagonal = lanes_of((32, 32)) == lax.broadcasted_iota(jnp.int32, (32, 32), 0)
    bias = 0.5 * jnp.sum(jnp.where(diagonal, square, 0.0), axis=1, keepdims=True)
    first = bias.astype(BF16).astype(F32)
    second = (bias - first).astype(BF16).astype(F32)
    lane = lanes_of((32, 128))
    extra = jnp.where(lane == 48, first, jnp.where(lane == 49, second, bias - first - second))
    for xo in range(8):
        moved = 0.5 * pltpu.roll(flat1[...], 4 * xo, 1)
        end = jnp.where((lane >= 48) & (lane < 51), extra, moved[:, 384:])
        band1_ref[pl.ds(xo * 32, 32), pl.ds(0, 384)] = moved[:, :384].astype(BF16)
        band1_ref[pl.ds(xo * 32, 32), pl.ds(384, 128)] = end.astype(BF16)
    for xo in range(6):
        for dz in range(3):
            tall[pl.ds(xo * 24, 24), pl.ds(dz * 256, 256)] = pltpu.roll(
                flat2[pl.ds(dz * 24, 24), :], 32 * xo, 1
            )
    band2_ref[...] = tall[...].astype(BF16)
    part = lanes_of((32, 240))
    along_z = (part < 48) | ((part >= 96) & (part < 144))
    div = div_ref[...].astype(F32)
    signed_ref[...] = jnp.where(along_z & (info_ref[2] == 1), -div, div).astype(BF16)


def slab(ref, start, pieces):
    for i, piece in enumerate(pieces):
        wide = piece.astype(F32)
        ref[pl.ds(start + i * 16, 16), :] = pltpu.roll(wide, 1, 1).astype(BF16)
        ref[pl.ds(start + 48 + i * 16, 16), :] = wide.astype(BF16)
        ref[pl.ds(start + 96 + i * 16, 16), :] = pltpu.roll(wide, 127, 1).astype(BF16)


def rows_of(even, a_ref, b_ref, start):
    a = a_ref[pl.ds(start, 16), :].astype(F32)
    b = b_ref[pl.ds(start, 16), :].astype(F32)
    return jnp.where(even, b, a), jnp.where(even, a, b)


def first_layer(first, second, band1_ref, pre_ref):
    ones = jnp.where(lax.broadcasted_iota(jnp.int32, (16, 256), 0) < 3, 1.0, 0.0).astype(BF16)
    rows = first if second is None else jnp.concatenate([first, second], axis=1)
    rows = jnp.concatenate([rows, ones[:, : rows.shape[1]]], axis=0)
    pre_ref[...] = jnp.dot(band1_ref[:, :448], rows, preferred_element_type=F32)


def activate(pre_ref, lanes, hidden_ref):
    scale = 2.0 * 0.7978845608028654
    for xo in range(8):
        at = pl.ds(xo * 32, 32)
        half = pre_ref[at, lanes]
        inner = half * (scale + (4.0 * 0.044715 * scale) * (half * half))
        hidden_ref[at, :] = (half + half * jnp.tanh(inner)).astype(BF16)


def level(hiddens, stress_ref, band2_ref):
    rows = jnp.concatenate(
        [jnp.concatenate([ref[...] for ref in refs], axis=0) for refs in hiddens], axis=1
    )
    result = jnp.dot(band2_ref[...], rows, preferred_element_type=F32)
    for n in range(len(hiddens)):
        sums = result[:, n * 128 : (n + 1) * 128]
        tiles = []
        for xo in range(6):
            at = xo * 24
            tiles.append(
                sums[at + 8 : at + 16]
                + pltpu.roll(sums[at : at + 8], 1, 1)
                + pltpu.roll(sums[at + 16 : at + 24], 127, 1)
            )
        stress_ref[n] = jnp.concatenate(tiles, axis=0).astype(BF16)


def forces_at(levels, div_ref, step):
    operands = []
    for below, here, above in levels:
        wide = here.astype(F32)
        before, after = pltpu.roll(wide, 1, 1).astype(BF16), pltpu.roll(wide, 127, 1).astype(BF16)
        operands.append(jnp.concatenate([below, here, above, before, after], axis=0))
    rows = jnp.concatenate(operands, axis=1)
    both = step * jnp.dot(div_ref[...], rows, preferred_element_type=F32)
    return [both[:, n * 128 : (n + 1) * 128] for n in range(len(levels))]


def halo_slab(message_ref, chip_even, group, columns, j):
    left_at, right_at = jnp.where(chip_even, 160, 112), jnp.where(chip_even, 112, 160)
    starts = [pl.multiple_of(at + group * 16, 16) for at in (left_at, 0, right_at)]
    slab(columns, j * 144, [message_ref[pl.ds(at, 16), :] for at in starts])


def end_term(q_ref, message_ref, z, x, sign, step):
    low = lax.broadcasted_iota(jnp.int32, (8, 128), 0) < 4
    face = message_ref[pl.ds(48 + (x // 2) * 16, 16), :].astype(F32)
    w = velocity(q_ref, z, x, 2, low)
    factor = step * viscosity + (sign * step) * w
    return factor * face[(x % 2) * 8 : (x % 2) * 8 + 8]


def half_of(pair, i):
    return pair[i // 2][(i % 2) * 8 : (i % 2) * 8 + 8]


def velocity(q_ref, z, x, c, low):
    first = jnp.broadcast_to(q_ref[z, x, c : c + 1, :], (8, 128))
    second = jnp.broadcast_to(q_ref[z, x, c + 4 : c + 5, :], (8, 128))
    return jnp.where(low, first, second)


def before_kernel(weights, *refs):
    keep_base, keep_state, step = weights
    info_ref, q_ref, coarse_ref, wide_a_ref, wide_b_ref, near_ref, band1_ref, band2_ref, div_ref = refs[:9]
    base_ref = refs[9] if keep_base else None
    columns, kept, stress, partial, hidden, pre = refs[-6:]
    chip_even = info_ref[1] == 0
    sign = jnp.where(info_ref[2] == 0, 1.0, -1.0)
    for j in range(4):
        left, right = rows_of(chip_even, wide_a_ref, wide_b_ref, j * 16)
        slab(columns, (3 + j) * 144, [left, coarse_ref[pl.ds(j * 16, 16), :], right])
    for i in range(3):
        halo_slab(near_ref, chip_even, 2 - i, columns, 7 + i)
    targets = [kept.at[0], kept.at[1], hidden.at[0], hidden.at[1], hidden.at[2]]
    for i, j in enumerate((3, 5)):
        rows = [columns[pl.ds((j + n) * 144, 432), :] for n in range(2)]
        first_layer(rows[0], rows[1], band1_ref, pre.at[i])
    first_layer(columns[pl.ds(7 * 144, 432), :], None, band1_ref, pre.at[2, :, pl.ds(0, 128)])
    for n, target in enumerate(targets):
        activate(pre.at[n // 2], pl.ds((n % 2) * 128, 128), target)
    level((targets[:3], targets[1:4]), stress.at[pl.ds(0, 2)], band2_ref)
    level((targets[2:],), stress.at[pl.ds(2, 1)], band2_ref)

    low = lax.broadcasted_iota(jnp.int32, (8, 128), 0) < 4
    sides = [rows_of(chip_even, wide_a_ref, wide_b_ref, 64 + z * 8) for z in range(0, 8, 2)]
    left, right = zip(*sides)
    for z in range(8):
        for x in range(8):
            here = q_ref[z, x]
            xp = q_ref[z, x + 1] if x < 7 else half_of(right, z)
            xm = q_ref[z, x - 1] if x > 0 else half_of(left, z)
            if z == 0:
                along_z, slope_z = q_ref[1, x], q_ref[1, x]
            elif z == 7:
                along_z, slope_z = q_ref[6, x], -q_ref[6, x]
            else:
                along_z = q_ref[z + 1, x] + q_ref[z - 1, x]
                slope_z = q_ref[z + 1, x] - q_ref[z - 1, x]
            swap = pltpu.roll(here, 4, 0)
            back, ahead = pltpu.roll(swap, 1, 1), pltpu.roll(swap, 127, 1)
            far = jnp.where(low, back, ahead)
            slope_y = jnp.where(low, swap - back, ahead - swap)
            spread = along_z + (xp + xm) + (swap + far)
            u, v, w = (velocity(q_ref, z, x, c, low) for c in range(3))
            advect = u * (xp - xm) + v * slope_y + sign * (w * slope_z)
            value = (keep_state - 6.0 * step * viscosity) * here
            value = value + (step * viscosity) * spread - (0.5 * step) * advect
            if keep_base:
                value = value + keep_base * base_ref[z, x]
            partial[z, x] = value

    (force,) = forces_at([[stress[0], stress[1], stress[2]]], div_ref, step)
    for z in (6, 7):
        for x in range(8):
            value = partial[z, x] + force[(x // 2) * 8 : (x // 2) * 8 + 8]
            if z == 7:
                value = value + end_term(q_ref, near_ref, z, x, -0.5 * sign, step)
            partial[z, x] = value


def after_body(
    step, info_ref, q_ref, own_columns, kept, near_stress, partial_ref, far_ref,
    band1_ref, band2_ref, div_ref, columns, stress, pre, hidden, new_ref,
):
    chip_even = info_ref[1] == 0
    sign = jnp.where(info_ref[2] == 0, 1.0, -1.0)
    for i in range(3):
        halo_slab(far_ref, chip_even, i, columns, 2 - i)
    hiddens = [hidden.at[0], hidden.at[1], hidden.at[2], kept.at[0], kept.at[1]]
    stresses = [stress.at[0], stress.at[1], stress.at[2], near_stress.at[0], near_stress.at[1]]

    def rows(j):
        halo = columns[pl.ds(j * 144, (3 - j) * 144), :]
        own = [own_columns[pl.ds(432, j * 144), :]] if j else []
        return jnp.concatenate([halo, *own], axis=0)

    first_layer(rows(1), rows(2), band1_ref, pre.at[0])
    first_layer(rows(0), None, band1_ref, pre.at[1, :, pl.ds(0, 128)])
    activate(pre.at[0], pl.ds(0, 128), hidden.at[1])
    activate(pre.at[0], pl.ds(128, 128), hidden.at[2])
    activate(pre.at[1], pl.ds(0, 128), hidden.at[0])
    level((hiddens[1:4], hiddens[2:5]), stress.at[pl.ds(1, 2)], band2_ref)
    level((hiddens[:3],), stress.at[pl.ds(0, 1)], band2_ref)

    for z in (6, 7):
        new_ref[z] = partial_ref[z]
    forces = forces_at([[ref[...] for ref in stresses[j : j + 3]] for j in range(3)], div_ref, step)
    for j in (2, 1, 0):
        for z in (2 * j, 2 * j + 1):
            for x in range(8):
                value = partial_ref[z, x] + forces[j][(x // 2) * 8 : (x // 2) * 8 + 8]
                if z == 0:
                    value = value + end_term(q_ref, far_ref, z, x, 0.5 * sign, step)
                new_ref[z, x] = value


def after_kernel(step, *refs):
    ins, outs, scratch = refs[:10], refs[10:15], refs[15:]
    after_body(step, *ins, *scratch, outs[0])
    emit_messages(ins[0], *outs)


def last_kernel(step, *refs):
    ins, outs, scratch, new = refs[:10], refs[10:12], refs[12:-1], refs[-1]
    core = ins[0][0]
    after_body(step, *ins, *scratch, new)
    for z in range(8):
        at = pl.ds(pl.multiple_of(jnp.where(ins[0][2] == 0, z, 7 - z) * 32, 32), 32)
        outs[0][at, :] = new[z, pl.ds(core * 4, 4)].reshape(32, 128)
        outs[1][at, :] = new[z, pl.ds((1 - core) * 4, 4)].reshape(32, 128)


def finish_kernel(info_ref, own_ref, other_ref, parity_ref, out_ref, native, flat):
    core = info_ref[0]
    lane = lanes_of((256, 128))
    low = jnp.where(core == 0, own_ref[...], other_ref[...])
    high = jnp.where(core == 0, other_ref[...], own_ref[...])
    native[...] = jnp.where(
        lane < HALF, pltpu.roll(low, 128 - EDGE, 1), pltpu.roll(high, HALF - EDGE, 1)
    )
    halves = [
        jnp.concatenate([native[pl.ds(p * 4 + c, 32, stride=8), :] for c in range(4)], axis=0)
        for p in range(2)
    ]
    split = lax.dot_general(
        thirds(jnp.concatenate(halves, axis=1)),
        parity_ref[...],
        (((1,), (1,)), ((), ())),
        preferred_element_type=F32,
    )
    flat[...] = split[:128] + split[128:256] + split[256:]
    for c in range(4):
        for z in range(8):
            out_ref[c, z] = flat[pl.ds((c * 8 + z) * 4, 4), :]


def chip_swap(value, odd):
    size = lax.axis_size("wide")
    pairs = []
    for i in range(size):
        chip, core = divmod(i, 2)
        to = chip + 1 if (chip + odd) % 2 == 0 else chip - 1
        pairs.append((i, (2 * to + core) % size))
    return lax.ppermute(value, "wide", pairs)


def net_swap(value, odd):
    size = lax.axis_size("net")
    pairs = [(i, (i + 1 if (i + odd) % 2 == 0 else i - 1) % size) for i in range(size)]
    return lax.ppermute(value, "net", pairs)


def partner(value):
    return lax.ppermute(value, "wide", [(i, i ^ 1) for i in range(lax.axis_size("wide"))])


def edge_shift(value, cross):
    wide, narrow = lax.axis_size("wide"), lax.axis_size("narrow")
    pairs = []
    for w in range(wide):
        for r in range(narrow):
            if cross:
                step, to = (-1 if w % 2 == 0 else 1), w ^ 1
            else:
                step, to = (1 if w % 2 == 0 else -1), w
            pairs.append((w * narrow + r, to * narrow + (r + step) % narrow))
    return lax.ppermute(value, ("wide", "narrow"), pairs)


def per_device(fields, conv1_weight, conv1_bias, conv2_weight):
    wide, net = lax.axis_index("wide"), lax.axis_index("net")
    info = jnp.stack([wide % 2, (wide // 2) % 2, net % 2]).astype(jnp.int32)
    native, same, cross, parity = call(
        pack_kernel,
        [((256, 128), F32), ((32, 128), F32), ((32, 128), F32), ((256, 256), BF16)],
        [pltpu.VMEM((128, 256), F32)],
        info, fields,
    )
    other = near(partner(native))
    same = near(edge_shift(same, False))
    cross = near(edge_shift(cross, True))
    fixed = call(
        weights_kernel,
        [((256, 512), BF16), ((144, 768), BF16), ((32, 240), BF16)],
        [pltpu.VMEM((32, 512), F32), pltpu.VMEM((72, 256), F32), pltpu.VMEM((144, 768), F32)],
        info, conv1_weight, conv2_weight, conv1_bias.reshape(1, 32),
        jnp.asarray(divergence_matrix(), BF16),
    )
    fixed = tuple(map(near, fixed))
    base, *messages = call(
        assemble_kernel,
        [((8, 8, 8, 128), F32)] + MESSAGES,
        [],
        info, near(native), other, same, cross, fixed[1],
    )
    state = base = near(base)
    stages = ((0.0, 1.0, time_step), (0.75, 0.25, 0.25 * time_step), (1.0 / 3.0, 2.0 / 3.0, 2.0 / 3.0 * time_step))
    scratch = [
        pltpu.VMEM((432, 128), BF16),
        pltpu.VMEM((3, 48, 128), BF16),
        pltpu.VMEM((2, 256, 256), F32),
        pltpu.VMEM((3, 256, 128), BF16),
    ]
    for stage, weights in enumerate(stages):
        wide_a, wide_b, net_a, net_b = messages
        got_a, got_b = chip_swap(wide_a, 0), chip_swap(wide_b, 1)
        rows_a, rows_b = [got_a[16:64], got_b[16:64]], [got_a[:48], got_b[:48]]
        far_a = net_swap(jnp.concatenate([net_a, *rows_a], axis=0), 0)
        far_b = net_swap(jnp.concatenate([net_b, *rows_b], axis=0), 1)
        before = call(
            functools.partial(before_kernel, weights),
            [((1440, 128), BF16), ((2, 256, 128), BF16), ((3, 48, 128), BF16), ((8, 8, 8, 128), F32)],
            [pltpu.VMEM((3, 256, 128), BF16), pltpu.VMEM((3, 256, 256), F32)],
            info, state, *map(near, (wide_a, got_a, got_b, far_a)), *fixed, *([base] if stage else []),
        )
        ins = (info, state, *map(near, before), near(far_b), *fixed)
        if stage < 2:
            state, *messages = call(
                functools.partial(after_kernel, weights[2]),
                [((8, 8, 8, 128), F32)] + MESSAGES,
                scratch,
                *ins,
            )
            state = near(state)
    own, away = call(
        functools.partial(last_kernel, stages[2][2]),
        [((256, 128), F32)] * 2,
        scratch + [pltpu.VMEM((8, 8, 8, 128), F32)],
        *ins,
    )
    return call(
        finish_kernel,
        None,
        [pltpu.VMEM((256, 128), F32), pltpu.VMEM((128, 256), F32)],
        info, near(own), near(partner(away)), near(parity),
        result=jax.ShapeDtypeStruct(fields.shape, F32),
    )


def solution(mesh):
    in_specs = (P(None, "net", "wide", "narrow"), P(), P(), P())
    out_specs = P(None, "net", "wide", "narrow")
    return jax.shard_map(
        per_device, mesh=mesh, in_specs=in_specs, out_specs=out_specs, check_vma=False
    )
```

```python
import functools

import jax
import jax.numpy as jnp
import numpy as np
from jax import lax
from jax.experimental import pallas as pl
from jax.experimental.pallas import tpu as pltpu
from jax.sharding import PartitionSpec as P

time_step = 0.2
viscosity = 0.05
EDGE = 9
HALF = 64
VMEM_LIMIT = 16 << 20
F32 = jnp.float32
BF16 = jnp.bfloat16
VM = pl.BlockSpec(memory_space=pltpu.VMEM)
SM = pl.BlockSpec(memory_space=pltpu.SMEM)


def divergence_matrix():
    m = np.zeros((4, 2, 4, 5, 6, 8), np.float32)
    sx, sy, sz = (0, 3, 4), (3, 1, 5), (4, 5, 2)
    for x in range(4):
        for comp in range(3):
            m[x, :, comp, 1, x + 2, sx[comp]] += 0.25
            m[x, :, comp, 1, x, sx[comp]] -= 0.25
            m[x, :, comp, 4, x + 1, sy[comp]] += 0.25
            m[x, :, comp, 3, x + 1, sy[comp]] -= 0.25
            m[x, :, comp, 2, x + 1, sz[comp]] += 0.25
            m[x, :, comp, 0, x + 1, sz[comp]] -= 0.25
    return m.reshape(32, 240)


def near(value):
    return pltpu.with_memory_space_constraint(value, pltpu.VMEM)


def call(kernel, outs, scratch, info, *args, result=None):
    return pl.pallas_call(
        kernel,
        out_shape=result or [pltpu.VMEM(s, d) for s, d in outs],
        in_specs=[SM] + [VM] * len(args),
        out_specs=VM if result else [VM] * len(outs),
        scratch_shapes=scratch,
        compiler_params=pltpu.CompilerParams(vmem_limit_bytes=VMEM_LIMIT),
    )(info, *args)


def lanes_of(shape):
    return lax.broadcasted_iota(jnp.int32, shape, len(shape) - 1)


def thirds(value):
    first = value.astype(BF16)
    rest = value - first.astype(F32)
    second = rest.astype(BF16)
    third = (rest - second.astype(F32)).astype(BF16)
    return jnp.concatenate([first, second, third], axis=0)


def pack_kernel(info_ref, fields_ref, native_ref, same_ref, cross_ref, parity_ref, flat):
    core = info_ref[0]
    row, col = lax.broadcasted_iota(jnp.int32, (256, 256), 0), lanes_of((256, 256))
    source = jnp.where(col < 128, 2 * col, 2 * col - 255)
    parity_ref[...] = jnp.where(row == source, 1.0, 0.0).astype(F32).astype(BF16)
    for c in range(4):
        for z in range(8):
            flat[pl.ds((c * 8 + z) * 4, 4), :] = fields_ref[c, z]
    split = jnp.dot(thirds(flat[...]), parity_ref[...], preferred_element_type=F32)
    parts = split[:128] + split[128:256] + split[256:]
    for p in range(2):
        for c in range(4):
            native_ref[pl.ds(p * 4 + c, 32, stride=8), :] = parts[
                c * 32 : (c + 1) * 32, p * 128 : (p + 1) * 128
            ]
    lane = lanes_of((32, 128))
    for out_ref, take_last in ((same_ref, core == 0), (cross_ref, core == 1)):
        offset = jnp.where(take_last, EDGE, 0)
        total = jnp.zeros((32, 128), F32)
        for g in range(8):
            moved = pltpu.roll(native_ref[pl.ds(g * 32, 32), :], g * 16 + offset, 1)
            total = jnp.where((lane >= g * 16) & (lane < g * 16 + EDGE), moved, total)
        out_ref[...] = total


def emit_messages(info_ref, q_ref, wide_a_ref, wide_b_ref, net_a_ref, net_b_ref):
    chip_even = info_ref[1] == 0
    low = lax.broadcasted_iota(jnp.int32, (8, 128), 0) < 4
    slabs = []
    for zc in range(4):
        means = []
        for xc in range(4):
            t = (q_ref[2 * zc, 2 * xc] + q_ref[2 * zc, 2 * xc + 1]) + (
                q_ref[2 * zc + 1, 2 * xc] + q_ref[2 * zc + 1, 2 * xc + 1]
            )
            means.append((t + pltpu.roll(t, 4, 0)) * 0.125)
        slab = jnp.concatenate(
            [jnp.where(low, means[0], means[1]), jnp.where(low, means[2], means[3])], axis=0
        )
        slabs.append(slab)
        wide_a_ref[pl.ds(zc * 16, 16), :] = slab.astype(BF16)
        wide_b_ref[pl.ds(zc * 16, 16), :] = slab.astype(BF16)
    for zc in range(3):
        at = pl.ds(zc * 16, 16)
        net_a_ref[at, :] = slabs[zc + 1].astype(BF16)
        net_b_ref[at, :] = slabs[zc].astype(BF16)
    xa, xb = jnp.where(chip_even, 7, 0), jnp.where(chip_even, 0, 7)
    for z in range(0, 8, 2):
        at = pl.ds(64 + z * 8, 16)
        wide_a_ref[at, :] = jnp.concatenate([q_ref[z, xa], q_ref[z + 1, xa]], axis=0).astype(BF16)
        wide_b_ref[at, :] = jnp.concatenate([q_ref[z, xb], q_ref[z + 1, xb]], axis=0).astype(BF16)
    for x in range(0, 8, 2):
        at = pl.ds(48 + x * 8, 16)
        net_a_ref[at, :] = jnp.concatenate([q_ref[7, x], q_ref[7, x + 1]], axis=0).astype(BF16)
        net_b_ref[at, :] = jnp.concatenate([q_ref[0, x], q_ref[0, x + 1]], axis=0).astype(BF16)


MESSAGES = [((128, 128), BF16), ((128, 128), BF16), ((112, 128), BF16), ((112, 128), BF16)]


def assemble_kernel(
    info_ref, own_ref, other_ref, same_ref, cross_ref, ready_ref,
    q_ref, wide_a_ref, wide_b_ref, net_a_ref, net_b_ref,
):
    core = info_ref[0]
    lane = lanes_of((32, 128))
    begin = jnp.where(core == 0, EDGE, 0)
    inside = (lane >= begin) & (lane < begin + HALF + EDGE)
    shift = jnp.where(core == 0, EDGE, HALF + EDGE)
    start = jnp.where(core == 0, 128, HALF + EDGE + 128)
    for block_ref, edge_ref, position in ((own_ref, same_ref, core), (other_ref, cross_ref, 1 - core)):
        edge = edge_ref[...]
        for g in range(8):
            block = pltpu.roll(block_ref[pl.ds(g * 32, 32), :], shift, 1)
            block = jnp.where(inside, block, pltpu.roll(edge, lax.rem(start - g * 16, 128), 1))
            q_ref[jnp.where(info_ref[2] == 0, g, 7 - g), pl.ds(position * 4, 4)] = block.reshape(4, 8, 128)
    emit_messages(info_ref, q_ref, wide_a_ref, wide_b_ref, net_a_ref, net_b_ref)


def weights_kernel(
    info_ref, w1_ref, w2_ref, b_ref, div_ref, band1_ref, band2_ref, signed_ref, flat1, flat2, tall
):
    flat1[...] = jnp.zeros_like(flat1)
    flat2[...] = jnp.zeros_like(flat2)
    for dz in range(3):
        for dx in range(3):
            for dy in range(3):
                tap = 9 * jnp.where(info_ref[2] == 0, dz, 2 - dz) + 3 * dx + dy
                flat1[:, pl.ds((dz * 3 + dy) * 48 + (1 + dx) * 4, 4)] = w1_ref[tap].astype(F32)
                flat2[pl.ds((dz * 3 + dy) * 8, 6), pl.ds(dx * 32, 32)] = w2_ref[tap].astype(F32)
    square = jnp.broadcast_to(b_ref[...], (32, 32))
    diagonal = lanes_of((32, 32)) == lax.broadcasted_iota(jnp.int32, (32, 32), 0)
    bias = 0.5 * jnp.sum(jnp.where(diagonal, square, 0.0), axis=1, keepdims=True)
    first = bias.astype(BF16).astype(F32)
    second = (bias - first).astype(BF16).astype(F32)
    lane = lanes_of((32, 128))
    extra = jnp.where(lane == 48, first, jnp.where(lane == 49, second, bias - first - second))
    for xo in range(8):
        moved = 0.5 * pltpu.roll(flat1[...], 4 * xo, 1)
        end = jnp.where((lane >= 48) & (lane < 51), extra, moved[:, 384:])
        band1_ref[pl.ds(xo * 32, 32), pl.ds(0, 384)] = moved[:, :384].astype(BF16)
        band1_ref[pl.ds(xo * 32, 32), pl.ds(384, 128)] = end.astype(BF16)
    for xo in range(6):
        for dz in range(3):
            tall[pl.ds(xo * 24, 24), pl.ds(dz * 256, 256)] = pltpu.roll(
                flat2[pl.ds(dz * 24, 24), :], 32 * xo, 1
            )
    band2_ref[...] = tall[...].astype(BF16)
    part = lanes_of((32, 240))
    along_z = (part < 48) | ((part >= 96) & (part < 144))
    div = div_ref[...].astype(F32)
    signed_ref[...] = jnp.where(along_z & (info_ref[2] == 1), -div, div).astype(BF16)


def slab(ref, start, pieces):
    for i, piece in enumerate(pieces):
        wide = piece.astype(F32)
        ref[pl.ds(start + i * 16, 16), :] = pltpu.roll(wide, 1, 1).astype(BF16)
        ref[pl.ds(start + 48 + i * 16, 16), :] = wide.astype(BF16)
        ref[pl.ds(start + 96 + i * 16, 16), :] = pltpu.roll(wide, 127, 1).astype(BF16)


def rows_of(even, a_ref, b_ref, start):
    a = a_ref[pl.ds(start, 16), :].astype(F32)
    b = b_ref[pl.ds(start, 16), :].astype(F32)
    return jnp.where(even, b, a), jnp.where(even, a, b)


def first_layer(first, second, band1_ref, pre_ref):
    ones = jnp.where(lax.broadcasted_iota(jnp.int32, (16, 256), 0) < 3, 1.0, 0.0).astype(BF16)
    rows = first if second is None else jnp.concatenate([first, second], axis=1)
    rows = jnp.concatenate([rows, ones[:, : rows.shape[1]]], axis=0)
    pre_ref[...] = jnp.dot(band1_ref[:, :448], rows, preferred_element_type=F32)


def activate(pre_ref, lanes, hidden_ref):
    scale = 2.0 * 0.7978845608028654
    for xo in range(8):
        at = pl.ds(xo * 32, 32)
        half = pre_ref[at, lanes]
        inner = half * (scale + (4.0 * 0.044715 * scale) * (half * half))
        hidden_ref[at, :] = (half + half * jnp.tanh(inner)).astype(BF16)


def level(hiddens, stress_ref, band2_ref):
    rows = jnp.concatenate(
        [jnp.concatenate([ref[...] for ref in refs], axis=0) for refs in hiddens], axis=1
    )
    result = jnp.dot(band2_ref[...], rows, preferred_element_type=F32)
    for n in range(len(hiddens)):
        sums = result[:, n * 128 : (n + 1) * 128]
        tiles = []
        for xo in range(6):
            at = xo * 24
            tiles.append(
                sums[at + 8 : at + 16]
                + pltpu.roll(sums[at : at + 8], 1, 1)
                + pltpu.roll(sums[at + 16 : at + 24], 127, 1)
            )
        stress_ref[n] = jnp.concatenate(tiles, axis=0).astype(BF16)


def forces_at(levels, div_ref, step):
    operands = []
    for below, here, above in levels:
        wide = here.astype(F32)
        before, after = pltpu.roll(wide, 1, 1).astype(BF16), pltpu.roll(wide, 127, 1).astype(BF16)
        operands.append(jnp.concatenate([below, here, above, before, after], axis=0))
    rows = jnp.concatenate(operands, axis=1)
    both = step * jnp.dot(div_ref[...], rows, preferred_element_type=F32)
    return [both[:, n * 128 : (n + 1) * 128] for n in range(len(levels))]


def halo_slab(message_ref, chip_even, group, columns, j):
    left_at, right_at = jnp.where(chip_even, 160, 112), jnp.where(chip_even, 112, 160)
    starts = [pl.multiple_of(at + group * 16, 16) for at in (left_at, 0, right_at)]
    slab(columns, j * 144, [message_ref[pl.ds(at, 16), :] for at in starts])


def end_term(q_ref, message_ref, z, x, sign, step):
    low = lax.broadcasted_iota(jnp.int32, (8, 128), 0) < 4
    face = message_ref[pl.ds(48 + (x // 2) * 16, 16), :].astype(F32)
    w = velocity(q_ref, z, x, 2, low)
    factor = step * viscosity + (sign * step) * w
    return factor * face[(x % 2) * 8 : (x % 2) * 8 + 8]


def half_of(pair, i):
    return pair[i // 2][(i % 2) * 8 : (i % 2) * 8 + 8]


def velocity(q_ref, z, x, c, low):
    first = jnp.broadcast_to(q_ref[z, x, c : c + 1, :], (8, 128))
    second = jnp.broadcast_to(q_ref[z, x, c + 4 : c + 5, :], (8, 128))
    return jnp.where(low, first, second)


def before_kernel(weights, *refs):
    keep_base, keep_state, step = weights
    info_ref, q_ref, coarse_ref, wide_a_ref, wide_b_ref, near_ref, band1_ref, band2_ref, div_ref = refs[:9]
    base_ref = refs[9] if keep_base else None
    columns, kept, stress, partial, hidden, pre = refs[-6:]
    chip_even = info_ref[1] == 0
    sign = jnp.where(info_ref[2] == 0, 1.0, -1.0)
    for j in range(4):
        left, right = rows_of(chip_even, wide_a_ref, wide_b_ref, j * 16)
        slab(columns, (3 + j) * 144, [left, coarse_ref[pl.ds(j * 16, 16), :], right])
    for i in range(3):
        halo_slab(near_ref, chip_even, 2 - i, columns, 7 + i)
    targets = [kept.at[0], kept.at[1], hidden.at[0], hidden.at[1], hidden.at[2]]
    for i, j in enumerate((3, 5)):
        rows = [columns[pl.ds((j + n) * 144, 432), :] for n in range(2)]
        first_layer(rows[0], rows[1], band1_ref, pre.at[i])
    first_layer(columns[pl.ds(7 * 144, 432), :], None, band1_ref, pre.at[2, :, pl.ds(0, 128)])
    for n, target in enumerate(targets):
        activate(pre.at[n // 2], pl.ds((n % 2) * 128, 128), target)
    level((targets[:3], targets[1:4]), stress.at[pl.ds(0, 2)], band2_ref)
    level((targets[2:],), stress.at[pl.ds(2, 1)], band2_ref)

    low = lax.broadcasted_iota(jnp.int32, (8, 128), 0) < 4
    sides = [rows_of(chip_even, wide_a_ref, wide_b_ref, 64 + z * 8) for z in range(0, 8, 2)]
    left, right = zip(*sides)
    for z in range(8):
        for x in range(8):
            here = q_ref[z, x]
            xp = q_ref[z, x + 1] if x < 7 else half_of(right, z)
            xm = q_ref[z, x - 1] if x > 0 else half_of(left, z)
            if z == 0:
                along_z, slope_z = q_ref[1, x], q_ref[1, x]
            elif z == 7:
                along_z, slope_z = q_ref[6, x], -q_ref[6, x]
            else:
                along_z = q_ref[z + 1, x] + q_ref[z - 1, x]
                slope_z = q_ref[z + 1, x] - q_ref[z - 1, x]
            swap = pltpu.roll(here, 4, 0)
            back, ahead = pltpu.roll(swap, 1, 1), pltpu.roll(swap, 127, 1)
            far = jnp.where(low, back, ahead)
            slope_y = jnp.where(low, swap - back, ahead - swap)
            spread = along_z + (xp + xm) + (swap + far)
            u, v, w = (velocity(q_ref, z, x, c, low) for c in range(3))
            advect = u * (xp - xm) + v * slope_y + sign * (w * slope_z)
            value = (keep_state - 6.0 * step * viscosity) * here
            value = value + (step * viscosity) * spread - (0.5 * step) * advect
            if keep_base:
                value = value + keep_base * base_ref[z, x]
            partial[z, x] = value

    (force,) = forces_at([[stress[0], stress[1], stress[2]]], div_ref, step)
    for z in (6, 7):
        for x in range(8):
            value = partial[z, x] + force[(x // 2) * 8 : (x // 2) * 8 + 8]
            if z == 7:
                value = value + end_term(q_ref, near_ref, z, x, -0.5 * sign, step)
            partial[z, x] = value


def after_body(
    step, info_ref, q_ref, own_columns, kept, near_stress, partial_ref, far_ref,
    band1_ref, band2_ref, div_ref, columns, stress, pre, hidden, new_ref,
):
    chip_even = info_ref[1] == 0
    sign = jnp.where(info_ref[2] == 0, 1.0, -1.0)
    for i in range(3):
        halo_slab(far_ref, chip_even, i, columns, 2 - i)
    hiddens = [hidden.at[0], hidden.at[1], hidden.at[2], kept.at[0], kept.at[1]]
    stresses = [stress.at[0], stress.at[1], stress.at[2], near_stress.at[0], near_stress.at[1]]

    def rows(j):
        halo = columns[pl.ds(j * 144, (3 - j) * 144), :]
        own = [own_columns[pl.ds(432, j * 144), :]] if j else []
        return jnp.concatenate([halo, *own], axis=0)

    first_layer(rows(1), rows(2), band1_ref, pre.at[0])
    first_layer(rows(0), None, band1_ref, pre.at[1, :, pl.ds(0, 128)])
    activate(pre.at[0], pl.ds(0, 128), hidden.at[1])
    activate(pre.at[0], pl.ds(128, 128), hidden.at[2])
    activate(pre.at[1], pl.ds(0, 128), hidden.at[0])
    level((hiddens[1:4], hiddens[2:5]), stress.at[pl.ds(1, 2)], band2_ref)
    level((hiddens[:3],), stress.at[pl.ds(0, 1)], band2_ref)

    for z in (6, 7):
        new_ref[z] = partial_ref[z]
    forces = forces_at([[ref[...] for ref in stresses[j : j + 3]] for j in range(3)], div_ref, step)
    for j in (2, 1, 0):
        for z in (2 * j, 2 * j + 1):
            for x in range(8):
                value = partial_ref[z, x] + forces[j][(x // 2) * 8 : (x // 2) * 8 + 8]
                if z == 0:
                    value = value + end_term(q_ref, far_ref, z, x, 0.5 * sign, step)
                new_ref[z, x] = value


def after_kernel(step, *refs):
    ins, outs, scratch = refs[:10], refs[10:15], refs[15:]
    after_body(step, *ins, *scratch, outs[0])
    emit_messages(ins[0], *outs)


def last_kernel(step, *refs):
    ins, outs, scratch, new = refs[:10], refs[10:12], refs[12:-1], refs[-1]
    core = ins[0][0]
    after_body(step, *ins, *scratch, new)
    for z in range(8):
        at = pl.ds(pl.multiple_of(jnp.where(ins[0][2] == 0, z, 7 - z) * 32, 32), 32)
        outs[0][at, :] = new[z, pl.ds(core * 4, 4)].reshape(32, 128)
    for t in range(4):
        low, high = (
            new[jnp.where(ins[0][2] == 0, z, 7 - z), pl.ds((1 - core) * 4, 4)].reshape(32, 128)
            for z in (2 * t, 2 * t + 1)
        )
        outs[1][pl.ds(t * 32, 32), :] = jnp.where(
            lanes_of((32, 128)) < HALF,
            pltpu.roll(low, 128 - EDGE, 1),
            pltpu.roll(high, HALF - EDGE, 1),
        )


def finish_kernel(info_ref, own_ref, other_ref, parity_ref, out_ref, native, flat):
    core = info_ref[0]
    lane = lanes_of((32, 128))
    begin = jnp.where(core == 0, 0, HALF)
    mine = (lane >= begin) & (lane < begin + HALF)
    shift = jnp.where(core == 0, 128 - EDGE, HALF - EDGE)
    for z in range(8):
        at = pl.ds(z * 32, 32)
        both = other_ref[pl.ds((z // 2) * 32, 32), :]
        swapped = pltpu.roll(both, HALF, 1)
        there = core == 0 if z % 2 == 0 else core == 1
        other = jnp.where(there, swapped, both)
        native[at, :] = jnp.where(mine, pltpu.roll(own_ref[at, :], shift, 1), other)
    halves = [
        jnp.concatenate([native[pl.ds(p * 4 + c, 32, stride=8), :] for c in range(4)], axis=0)
        for p in range(2)
    ]
    split = lax.dot_general(
        thirds(jnp.concatenate(halves, axis=1)),
        parity_ref[...],
        (((1,), (1,)), ((), ())),
        preferred_element_type=F32,
    )
    flat[...] = split[:128] + split[128:256] + split[256:]
    for c in range(4):
        for z in range(8):
            out_ref[c, z] = flat[pl.ds((c * 8 + z) * 4, 4), :]


def chip_swap(value, odd):
    size = lax.axis_size("wide")
    pairs = []
    for i in range(size):
        chip, core = divmod(i, 2)
        to = chip + 1 if (chip + odd) % 2 == 0 else chip - 1
        pairs.append((i, (2 * to + core) % size))
    return lax.ppermute(value, "wide", pairs)


def net_swap(value, odd):
    size = lax.axis_size("net")
    pairs = [(i, (i + 1 if (i + odd) % 2 == 0 else i - 1) % size) for i in range(size)]
    return lax.ppermute(value, "net", pairs)


def partner(value):
    return lax.ppermute(value, "wide", [(i, i ^ 1) for i in range(lax.axis_size("wide"))])


def edge_shift(value, cross):
    wide, narrow = lax.axis_size("wide"), lax.axis_size("narrow")
    pairs = []
    for w in range(wide):
        for r in range(narrow):
            if cross:
                step, to = (-1 if w % 2 == 0 else 1), w ^ 1
            else:
                step, to = (1 if w % 2 == 0 else -1), w
            pairs.append((w * narrow + r, to * narrow + (r + step) % narrow))
    return lax.ppermute(value, ("wide", "narrow"), pairs)


def per_device(fields, conv1_weight, conv1_bias, conv2_weight):
    wide, net = lax.axis_index("wide"), lax.axis_index("net")
    info = jnp.stack([wide % 2, (wide // 2) % 2, net % 2]).astype(jnp.int32)
    native, same, cross, parity = call(
        pack_kernel,
        [((256, 128), F32), ((32, 128), F32), ((32, 128), F32), ((256, 256), BF16)],
        [pltpu.VMEM((128, 256), F32)],
        info, fields,
    )
    other = near(partner(native))
    same = near(edge_shift(same, False))
    cross = near(edge_shift(cross, True))
    fixed = call(
        weights_kernel,
        [((256, 512), BF16), ((144, 768), BF16), ((32, 240), BF16)],
        [pltpu.VMEM((32, 512), F32), pltpu.VMEM((72, 256), F32), pltpu.VMEM((144, 768), F32)],
        info, conv1_weight, conv2_weight, conv1_bias.reshape(1, 32),
        jnp.asarray(divergence_matrix(), BF16),
    )
    fixed = tuple(map(near, fixed))
    base, *messages = call(
        assemble_kernel,
        [((8, 8, 8, 128), F32)] + MESSAGES,
        [],
        info, near(native), other, same, cross, fixed[1],
    )
    state = base = near(base)
    stages = ((0.0, 1.0, time_step), (0.75, 0.25, 0.25 * time_step), (1.0 / 3.0, 2.0 / 3.0, 2.0 / 3.0 * time_step))
    scratch = [
        pltpu.VMEM((432, 128), BF16),
        pltpu.VMEM((3, 48, 128), BF16),
        pltpu.VMEM((2, 256, 256), F32),
        pltpu.VMEM((3, 256, 128), BF16),
    ]
    for stage, weights in enumerate(stages):
        wide_a, wide_b, net_a, net_b = messages
        got_a, got_b = chip_swap(wide_a, 0), chip_swap(wide_b, 1)
        rows_a, rows_b = [got_a[16:64], got_b[16:64]], [got_a[:48], got_b[:48]]
        far_a = net_swap(jnp.concatenate([net_a, *rows_a], axis=0), 0)
        far_b = net_swap(jnp.concatenate([net_b, *rows_b], axis=0), 1)
        before = call(
            functools.partial(before_kernel, weights),
            [((1440, 128), BF16), ((2, 256, 128), BF16), ((3, 48, 128), BF16), ((8, 8, 8, 128), F32)],
            [pltpu.VMEM((3, 256, 128), BF16), pltpu.VMEM((3, 256, 256), F32)],
            info, state, *map(near, (wide_a, got_a, got_b, far_a)), *fixed, *([base] if stage else []),
        )
        ins = (info, state, *map(near, before), near(far_b), *fixed)
        if stage < 2:
            state, *messages = call(
                functools.partial(after_kernel, weights[2]),
                [((8, 8, 8, 128), F32)] + MESSAGES,
                scratch,
                *ins,
            )
            state = near(state)
    own, away = call(
        functools.partial(last_kernel, stages[2][2]),
        [((256, 128), F32), ((128, 128), F32)],
        scratch + [pltpu.VMEM((8, 8, 8, 128), F32)],
        *ins,
    )
    return call(
        finish_kernel,
        None,
        [pltpu.VMEM((256, 128), F32), pltpu.VMEM((128, 256), F32)],
        info, near(own), near(partner(away)), near(parity),
        result=jax.ShapeDtypeStruct(fields.shape, F32),
    )


def solution(mesh):
    in_specs = (P(None, "net", "wide", "narrow"), P(), P(), P())
    out_specs = P(None, "net", "wide", "narrow")
    return jax.shard_map(
        per_device, mesh=mesh, in_specs=in_specs, out_specs=out_specs, check_vma=False
    )
```

```python
import functools

import jax
import jax.numpy as jnp
import numpy as np
from jax import lax
from jax.experimental import pallas as pl
from jax.experimental.pallas import tpu as pltpu
from jax.sharding import PartitionSpec as P

time_step = 0.2
viscosity = 0.05
EDGE = 9
HALF = 64
VMEM_LIMIT = 16 << 20
F32 = jnp.float32
BF16 = jnp.bfloat16
VM = pl.BlockSpec(memory_space=pltpu.VMEM)
SM = pl.BlockSpec(memory_space=pltpu.SMEM)


def divergence_matrix():
    m = np.zeros((4, 2, 4, 5, 6, 8), np.float32)
    sx, sy, sz = (0, 3, 4), (3, 1, 5), (4, 5, 2)
    for x in range(4):
        for comp in range(3):
            m[x, :, comp, 1, x + 2, sx[comp]] += 0.25
            m[x, :, comp, 1, x, sx[comp]] -= 0.25
            m[x, :, comp, 4, x + 1, sy[comp]] += 0.25
            m[x, :, comp, 3, x + 1, sy[comp]] -= 0.25
            m[x, :, comp, 2, x + 1, sz[comp]] += 0.25
            m[x, :, comp, 0, x + 1, sz[comp]] -= 0.25
    return m.reshape(32, 240)


def near(value):
    return pltpu.with_memory_space_constraint(value, pltpu.VMEM)


def call(kernel, outs, scratch, info, *args, result=None):
    return pl.pallas_call(
        kernel,
        out_shape=result or [pltpu.VMEM(s, d) for s, d in outs],
        in_specs=[SM] + [VM] * len(args),
        out_specs=pl.BlockSpec(memory_space=pltpu.HBM) if result else [VM] * len(outs),
        scratch_shapes=scratch,
        compiler_params=pltpu.CompilerParams(vmem_limit_bytes=VMEM_LIMIT),
    )(info, *args)


def lanes_of(shape):
    return lax.broadcasted_iota(jnp.int32, shape, len(shape) - 1)


def thirds(value):
    first = value.astype(BF16)
    rest = value - first.astype(F32)
    second = rest.astype(BF16)
    third = (rest - second.astype(F32)).astype(BF16)
    return jnp.concatenate([first, second, third], axis=0)


def pack_kernel(info_ref, fields_ref, native_ref, same_ref, cross_ref, parity_ref, flat):
    core = info_ref[0]
    row, col = lax.broadcasted_iota(jnp.int32, (256, 256), 0), lanes_of((256, 256))
    source = jnp.where(col < 128, 2 * col, 2 * col - 255)
    parity_ref[...] = jnp.where(row == source, 1.0, 0.0).astype(F32).astype(BF16)
    for c in range(4):
        for z in range(8):
            flat[pl.ds((c * 8 + z) * 4, 4), :] = fields_ref[c, z]
    split = jnp.dot(thirds(flat[...]), parity_ref[...], preferred_element_type=F32)
    parts = split[:128] + split[128:256] + split[256:]
    for p in range(2):
        for c in range(4):
            native_ref[pl.ds(p * 4 + c, 32, stride=8), :] = parts[
                c * 32 : (c + 1) * 32, p * 128 : (p + 1) * 128
            ]
    lane = lanes_of((32, 128))
    for out_ref, take_last in ((same_ref, core == 0), (cross_ref, core == 1)):
        offset = jnp.where(take_last, EDGE, 0)
        total = jnp.zeros((32, 128), F32)
        for g in range(8):
            moved = pltpu.roll(native_ref[pl.ds(g * 32, 32), :], g * 16 + offset, 1)
            total = jnp.where((lane >= g * 16) & (lane < g * 16 + EDGE), moved, total)
        out_ref[...] = total


def emit_messages(info_ref, q_ref, wide_a_ref, wide_b_ref, net_a_ref, net_b_ref):
    chip_even = info_ref[1] == 0
    low = lax.broadcasted_iota(jnp.int32, (8, 128), 0) < 4
    slabs = []
    for zc in range(4):
        means = []
        for xc in range(4):
            t = (q_ref[2 * zc, 2 * xc] + q_ref[2 * zc, 2 * xc + 1]) + (
                q_ref[2 * zc + 1, 2 * xc] + q_ref[2 * zc + 1, 2 * xc + 1]
            )
            means.append((t + pltpu.roll(t, 4, 0)) * 0.125)
        slab = jnp.concatenate(
            [jnp.where(low, means[0], means[1]), jnp.where(low, means[2], means[3])], axis=0
        )
        slabs.append(slab)
        wide_a_ref[pl.ds(zc * 16, 16), :] = slab.astype(BF16)
        wide_b_ref[pl.ds(zc * 16, 16), :] = slab.astype(BF16)
    for zc in range(3):
        at = pl.ds(zc * 16, 16)
        net_a_ref[at, :] = slabs[zc + 1].astype(BF16)
        net_b_ref[at, :] = slabs[zc].astype(BF16)
    xa, xb = jnp.where(chip_even, 7, 0), jnp.where(chip_even, 0, 7)
    for z in range(0, 8, 2):
        at = pl.ds(64 + z * 8, 16)
        wide_a_ref[at, :] = jnp.concatenate([q_ref[z, xa], q_ref[z + 1, xa]], axis=0).astype(BF16)
        wide_b_ref[at, :] = jnp.concatenate([q_ref[z, xb], q_ref[z + 1, xb]], axis=0).astype(BF16)
    for x in range(0, 8, 2):
        at = pl.ds(48 + x * 8, 16)
        net_a_ref[at, :] = jnp.concatenate([q_ref[7, x], q_ref[7, x + 1]], axis=0).astype(BF16)
        net_b_ref[at, :] = jnp.concatenate([q_ref[0, x], q_ref[0, x + 1]], axis=0).astype(BF16)


MESSAGES = [((128, 128), BF16), ((128, 128), BF16), ((112, 128), BF16), ((112, 128), BF16)]


def assemble_kernel(
    info_ref, own_ref, other_ref, same_ref, cross_ref, ready_ref,
    q_ref, wide_a_ref, wide_b_ref, net_a_ref, net_b_ref,
):
    core = info_ref[0]
    lane = lanes_of((32, 128))
    begin = jnp.where(core == 0, EDGE, 0)
    inside = (lane >= begin) & (lane < begin + HALF + EDGE)
    shift = jnp.where(core == 0, EDGE, HALF + EDGE)
    start = jnp.where(core == 0, 128, HALF + EDGE + 128)
    for block_ref, edge_ref, position in ((own_ref, same_ref, core), (other_ref, cross_ref, 1 - core)):
        edge = edge_ref[...]
        for g in range(8):
            block = pltpu.roll(block_ref[pl.ds(g * 32, 32), :], shift, 1)
            block = jnp.where(inside, block, pltpu.roll(edge, lax.rem(start - g * 16, 128), 1))
            q_ref[jnp.where(info_ref[2] == 0, g, 7 - g), pl.ds(position * 4, 4)] = block.reshape(4, 8, 128)
    emit_messages(info_ref, q_ref, wide_a_ref, wide_b_ref, net_a_ref, net_b_ref)


def weights_kernel(
    info_ref, w1_ref, w2_ref, b_ref, div_ref, band1_ref, band2_ref, signed_ref, flat1, flat2, tall
):
    flat1[...] = jnp.zeros_like(flat1)
    flat2[...] = jnp.zeros_like(flat2)
    for dz in range(3):
        for dx in range(3):
            for dy in range(3):
                tap = 9 * jnp.where(info_ref[2] == 0, dz, 2 - dz) + 3 * dx + dy
                flat1[:, pl.ds((dz * 3 + dy) * 48 + (1 + dx) * 4, 4)] = w1_ref[tap].astype(F32)
                flat2[pl.ds((dz * 3 + dy) * 8, 6), pl.ds(dx * 32, 32)] = w2_ref[tap].astype(F32)
    square = jnp.broadcast_to(b_ref[...], (32, 32))
    diagonal = lanes_of((32, 32)) == lax.broadcasted_iota(jnp.int32, (32, 32), 0)
    bias = 0.5 * jnp.sum(jnp.where(diagonal, square, 0.0), axis=1, keepdims=True)
    first = bias.astype(BF16).astype(F32)
    second = (bias - first).astype(BF16).astype(F32)
    lane = lanes_of((32, 128))
    extra = jnp.where(lane == 48, first, jnp.where(lane == 49, second, bias - first - second))
    for xo in range(8):
        moved = 0.5 * pltpu.roll(flat1[...], 4 * xo, 1)
        end = jnp.where((lane >= 48) & (lane < 51), extra, moved[:, 384:])
        band1_ref[pl.ds(xo * 32, 32), pl.ds(0, 384)] = moved[:, :384].astype(BF16)
        band1_ref[pl.ds(xo * 32, 32), pl.ds(384, 128)] = end.astype(BF16)
    for xo in range(6):
        for dz in range(3):
            tall[pl.ds(xo * 24, 24), pl.ds(dz * 256, 256)] = pltpu.roll(
                flat2[pl.ds(dz * 24, 24), :], 32 * xo, 1
            )
    band2_ref[...] = tall[...].astype(BF16)
    part = lanes_of((32, 240))
    along_z = (part < 48) | ((part >= 96) & (part < 144))
    div = div_ref[...].astype(F32)
    signed_ref[...] = jnp.where(along_z & (info_ref[2] == 1), -div, div).astype(BF16)


def slab(ref, start, pieces):
    for i, piece in enumerate(pieces):
        wide = piece.astype(F32)
        ref[pl.ds(start + i * 16, 16), :] = pltpu.roll(wide, 1, 1).astype(BF16)
        ref[pl.ds(start + 48 + i * 16, 16), :] = wide.astype(BF16)
        ref[pl.ds(start + 96 + i * 16, 16), :] = pltpu.roll(wide, 127, 1).astype(BF16)


def rows_of(even, a_ref, b_ref, start):
    a = a_ref[pl.ds(start, 16), :].astype(F32)
    b = b_ref[pl.ds(start, 16), :].astype(F32)
    return jnp.where(even, b, a), jnp.where(even, a, b)


def first_layer(first, second, band1_ref, pre_ref):
    ones = jnp.where(lax.broadcasted_iota(jnp.int32, (16, 256), 0) < 3, 1.0, 0.0).astype(BF16)
    rows = first if second is None else jnp.concatenate([first, second], axis=1)
    rows = jnp.concatenate([rows, ones[:, : rows.shape[1]]], axis=0)
    pre_ref[...] = jnp.dot(band1_ref[:, :448], rows, preferred_element_type=F32)


def activate(pre_ref, lanes, hidden_ref):
    scale = 2.0 * 0.7978845608028654
    for xo in range(8):
        at = pl.ds(xo * 32, 32)
        half = pre_ref[at, lanes]
        inner = half * (scale + (4.0 * 0.044715 * scale) * (half * half))
        hidden_ref[at, :] = (half + half * jnp.tanh(inner)).astype(BF16)


def level(hiddens, stress_ref, band2_ref):
    rows = jnp.concatenate(
        [jnp.concatenate([ref[...] for ref in refs], axis=0) for refs in hiddens], axis=1
    )
    result = jnp.dot(band2_ref[...], rows, preferred_element_type=F32)
    for n in range(len(hiddens)):
        sums = result[:, n * 128 : (n + 1) * 128]
        tiles = []
        for xo in range(6):
            at = xo * 24
            tiles.append(
                sums[at + 8 : at + 16]
                + pltpu.roll(sums[at : at + 8], 1, 1)
                + pltpu.roll(sums[at + 16 : at + 24], 127, 1)
            )
        stress_ref[n] = jnp.concatenate(tiles, axis=0).astype(BF16)


def forces_at(levels, div_ref, step):
    operands = []
    for below, here, above in levels:
        wide = here.astype(F32)
        before, after = pltpu.roll(wide, 1, 1).astype(BF16), pltpu.roll(wide, 127, 1).astype(BF16)
        operands.append(jnp.concatenate([below, here, above, before, after], axis=0))
    rows = jnp.concatenate(operands, axis=1)
    both = step * jnp.dot(div_ref[...], rows, preferred_element_type=F32)
    return [both[:, n * 128 : (n + 1) * 128] for n in range(len(levels))]


def halo_slab(message_ref, chip_even, group, columns, j):
    left_at, right_at = jnp.where(chip_even, 160, 112), jnp.where(chip_even, 112, 160)
    starts = [pl.multiple_of(at + group * 16, 16) for at in (left_at, 0, right_at)]
    slab(columns, j * 144, [message_ref[pl.ds(at, 16), :] for at in starts])


def end_term(q_ref, message_ref, z, x, sign, step):
    low = lax.broadcasted_iota(jnp.int32, (8, 128), 0) < 4
    face = message_ref[pl.ds(48 + (x // 2) * 16, 16), :].astype(F32)
    w = velocity(q_ref, z, x, 2, low)
    factor = step * viscosity + (sign * step) * w
    return factor * face[(x % 2) * 8 : (x % 2) * 8 + 8]


def half_of(pair, i):
    return pair[i // 2][(i % 2) * 8 : (i % 2) * 8 + 8]


def velocity(q_ref, z, x, c, low):
    first = jnp.broadcast_to(q_ref[z, x, c : c + 1, :], (8, 128))
    second = jnp.broadcast_to(q_ref[z, x, c + 4 : c + 5, :], (8, 128))
    return jnp.where(low, first, second)


def before_kernel(weights, *refs):
    keep_base, keep_state, step = weights
    info_ref, q_ref, coarse_ref, wide_a_ref, wide_b_ref, near_ref, band1_ref, band2_ref, div_ref = refs[:9]
    base_ref = refs[9] if keep_base else None
    columns, kept, stress, partial, hidden, pre = refs[-6:]
    chip_even = info_ref[1] == 0
    sign = jnp.where(info_ref[2] == 0, 1.0, -1.0)
    for j in range(4):
        left, right = rows_of(chip_even, wide_a_ref, wide_b_ref, j * 16)
        slab(columns, (3 + j) * 144, [left, coarse_ref[pl.ds(j * 16, 16), :], right])
    for i in range(3):
        halo_slab(near_ref, chip_even, 2 - i, columns, 7 + i)
    targets = [kept.at[0], kept.at[1], hidden.at[0], hidden.at[1], hidden.at[2]]
    for i, j in enumerate((3, 5)):
        rows = [columns[pl.ds((j + n) * 144, 432), :] for n in range(2)]
        first_layer(rows[0], rows[1], band1_ref, pre.at[i])
    first_layer(columns[pl.ds(7 * 144, 432), :], None, band1_ref, pre.at[2, :, pl.ds(0, 128)])
    for n, target in enumerate(targets):
        activate(pre.at[n // 2], pl.ds((n % 2) * 128, 128), target)
    level((targets[:3], targets[1:4]), stress.at[pl.ds(0, 2)], band2_ref)
    level((targets[2:],), stress.at[pl.ds(2, 1)], band2_ref)

    low = lax.broadcasted_iota(jnp.int32, (8, 128), 0) < 4
    sides = [rows_of(chip_even, wide_a_ref, wide_b_ref, 64 + z * 8) for z in range(0, 8, 2)]
    left, right = zip(*sides)
    for z in range(8):
        for x in range(8):
            here = q_ref[z, x]
            xp = q_ref[z, x + 1] if x < 7 else half_of(right, z)
            xm = q_ref[z, x - 1] if x > 0 else half_of(left, z)
            if z == 0:
                along_z, slope_z = q_ref[1, x], q_ref[1, x]
            elif z == 7:
                along_z, slope_z = q_ref[6, x], -q_ref[6, x]
            else:
                along_z = q_ref[z + 1, x] + q_ref[z - 1, x]
                slope_z = q_ref[z + 1, x] - q_ref[z - 1, x]
            swap = pltpu.roll(here, 4, 0)
            back, ahead = pltpu.roll(swap, 1, 1), pltpu.roll(swap, 127, 1)
            far = jnp.where(low, back, ahead)
            slope_y = jnp.where(low, swap - back, ahead - swap)
            spread = along_z + (xp + xm) + (swap + far)
            u, v, w = (velocity(q_ref, z, x, c, low) for c in range(3))
            advect = u * (xp - xm) + v * slope_y + sign * (w * slope_z)
            value = (keep_state - 6.0 * step * viscosity) * here
            value = value + (step * viscosity) * spread - (0.5 * step) * advect
            if keep_base:
                value = value + keep_base * base_ref[z, x]
            partial[z, x] = value

    (force,) = forces_at([[stress[0], stress[1], stress[2]]], div_ref, step)
    for z in (6, 7):
        for x in range(8):
            value = partial[z, x] + force[(x // 2) * 8 : (x // 2) * 8 + 8]
            if z == 7:
                value = value + end_term(q_ref, near_ref, z, x, -0.5 * sign, step)
            partial[z, x] = value


def after_body(
    step, info_ref, q_ref, own_columns, kept, near_stress, partial_ref, far_ref,
    band1_ref, band2_ref, div_ref, columns, stress, pre, hidden, new_ref,
):
    chip_even = info_ref[1] == 0
    sign = jnp.where(info_ref[2] == 0, 1.0, -1.0)
    for i in range(3):
        halo_slab(far_ref, chip_even, i, columns, 2 - i)
    hiddens = [hidden.at[0], hidden.at[1], hidden.at[2], kept.at[0], kept.at[1]]
    stresses = [stress.at[0], stress.at[1], stress.at[2], near_stress.at[0], near_stress.at[1]]

    def rows(j):
        halo = columns[pl.ds(j * 144, (3 - j) * 144), :]
        own = [own_columns[pl.ds(432, j * 144), :]] if j else []
        return jnp.concatenate([halo, *own], axis=0)

    first_layer(rows(1), rows(2), band1_ref, pre.at[0])
    first_layer(rows(0), None, band1_ref, pre.at[1, :, pl.ds(0, 128)])
    activate(pre.at[0], pl.ds(0, 128), hidden.at[1])
    activate(pre.at[0], pl.ds(128, 128), hidden.at[2])
    activate(pre.at[1], pl.ds(0, 128), hidden.at[0])
    level((hiddens[1:4], hiddens[2:5]), stress.at[pl.ds(1, 2)], band2_ref)
    level((hiddens[:3],), stress.at[pl.ds(0, 1)], band2_ref)

    for z in (6, 7):
        new_ref[z] = partial_ref[z]
    forces = forces_at([[ref[...] for ref in stresses[j : j + 3]] for j in range(3)], div_ref, step)
    for j in (2, 1, 0):
        for z in (2 * j, 2 * j + 1):
            for x in range(8):
                value = partial_ref[z, x] + forces[j][(x // 2) * 8 : (x // 2) * 8 + 8]
                if z == 0:
                    value = value + end_term(q_ref, far_ref, z, x, 0.5 * sign, step)
                new_ref[z, x] = value


def after_kernel(step, *refs):
    ins, outs, scratch = refs[:10], refs[10:15], refs[15:]
    after_body(step, *ins, *scratch, outs[0])
    emit_messages(ins[0], *outs)


def last_kernel(step, *refs):
    ins, outs, scratch, new = refs[:10], refs[10:12], refs[12:-1], refs[-1]
    core = ins[0][0]
    after_body(step, *ins, *scratch, new)
    for z in range(8):
        at = pl.ds(pl.multiple_of(jnp.where(ins[0][2] == 0, z, 7 - z) * 32, 32), 32)
        outs[0][at, :] = new[z, pl.ds(core * 4, 4)].reshape(32, 128)
        outs[1][at, :] = new[z, pl.ds((1 - core) * 4, 4)].reshape(32, 128)


def finish_kernel(info_ref, own_ref, other_ref, parity_ref, out_far, native, flat, out_ref, sems):
    core = info_ref[0]
    lane = lanes_of((256, 128))
    low = jnp.where(core == 0, own_ref[...], other_ref[...])
    high = jnp.where(core == 0, other_ref[...], own_ref[...])
    native[...] = jnp.where(
        lane < HALF, pltpu.roll(low, 128 - EDGE, 1), pltpu.roll(high, HALF - EDGE, 1)
    )
    copies = []
    for c in range(4):
        halves = [native[pl.ds(p * 4 + c, 32, stride=8), :] for p in range(2)]
        split = lax.dot_general(
            thirds(jnp.concatenate(halves, axis=1)),
            parity_ref[...],
            (((1,), (1,)), ((), ())),
            preferred_element_type=F32,
        )
        flat[pl.ds(c * 32, 32), :] = split[:32] + split[32:64] + split[64:]
        for z in range(8):
            out_ref[c, z] = flat[pl.ds((c * 8 + z) * 4, 4), :]
        copies.append(pltpu.make_async_copy(out_ref.at[c], out_far.at[c], sems.at[c]))
        copies[c].start()
    for copy in copies:
        copy.wait()


def chip_swap(value, odd):
    size = lax.axis_size("wide")
    pairs = []
    for i in range(size):
        chip, core = divmod(i, 2)
        to = chip + 1 if (chip + odd) % 2 == 0 else chip - 1
        pairs.append((i, (2 * to + core) % size))
    return lax.ppermute(value, "wide", pairs)


def net_swap(value, odd):
    size = lax.axis_size("net")
    pairs = [(i, (i + 1 if (i + odd) % 2 == 0 else i - 1) % size) for i in range(size)]
    return lax.ppermute(value, "net", pairs)


def partner(value):
    return lax.ppermute(value, "wide", [(i, i ^ 1) for i in range(lax.axis_size("wide"))])


def edge_shift(value, cross):
    wide, narrow = lax.axis_size("wide"), lax.axis_size("narrow")
    pairs = []
    for w in range(wide):
        for r in range(narrow):
            if cross:
                step, to = (-1 if w % 2 == 0 else 1), w ^ 1
            else:
                step, to = (1 if w % 2 == 0 else -1), w
            pairs.append((w * narrow + r, to * narrow + (r + step) % narrow))
    return lax.ppermute(value, ("wide", "narrow"), pairs)


def per_device(fields, conv1_weight, conv1_bias, conv2_weight):
    wide, net = lax.axis_index("wide"), lax.axis_index("net")
    info = jnp.stack([wide % 2, (wide // 2) % 2, net % 2]).astype(jnp.int32)
    native, same, cross, parity = call(
        pack_kernel,
        [((256, 128), F32), ((32, 128), F32), ((32, 128), F32), ((256, 256), BF16)],
        [pltpu.VMEM((128, 256), F32)],
        info, fields,
    )
    other = near(partner(native))
    same = near(edge_shift(same, False))
    cross = near(edge_shift(cross, True))
    fixed = call(
        weights_kernel,
        [((256, 512), BF16), ((144, 768), BF16), ((32, 240), BF16)],
        [pltpu.VMEM((32, 512), F32), pltpu.VMEM((72, 256), F32), pltpu.VMEM((144, 768), F32)],
        info, conv1_weight, conv2_weight, conv1_bias.reshape(1, 32),
        jnp.asarray(divergence_matrix(), BF16),
    )
    fixed = tuple(map(near, fixed))
    base, *messages = call(
        assemble_kernel,
        [((8, 8, 8, 128), F32)] + MESSAGES,
        [],
        info, near(native), other, same, cross, fixed[1],
    )
    state = base = near(base)
    stages = ((0.0, 1.0, time_step), (0.75, 0.25, 0.25 * time_step), (1.0 / 3.0, 2.0 / 3.0, 2.0 / 3.0 * time_step))
    scratch = [
        pltpu.VMEM((432, 128), BF16),
        pltpu.VMEM((3, 48, 128), BF16),
        pltpu.VMEM((2, 256, 256), F32),
        pltpu.VMEM((3, 256, 128), BF16),
    ]
    for stage, weights in enumerate(stages):
        wide_a, wide_b, net_a, net_b = messages
        got_a, got_b = chip_swap(wide_a, 0), chip_swap(wide_b, 1)
        rows_a, rows_b = [got_a[16:64], got_b[16:64]], [got_a[:48], got_b[:48]]
        far_a = net_swap(jnp.concatenate([net_a, *rows_a], axis=0), 0)
        far_b = net_swap(jnp.concatenate([net_b, *rows_b], axis=0), 1)
        before = call(
            functools.partial(before_kernel, weights),
            [((1440, 128), BF16), ((2, 256, 128), BF16), ((3, 48, 128), BF16), ((8, 8, 8, 128), F32)],
            [pltpu.VMEM((3, 256, 128), BF16), pltpu.VMEM((3, 256, 256), F32)],
            info, state, *map(near, (wide_a, got_a, got_b, far_a)), *fixed, *([base] if stage else []),
        )
        ins = (info, state, *map(near, before), near(far_b), *fixed)
        if stage < 2:
            state, *messages = call(
                functools.partial(after_kernel, weights[2]),
                [((8, 8, 8, 128), F32)] + MESSAGES,
                scratch,
                *ins,
            )
            state = near(state)
    own, away = call(
        functools.partial(last_kernel, stages[2][2]),
        [((256, 128), F32)] * 2,
        scratch + [pltpu.VMEM((8, 8, 8, 128), F32)],
        *ins,
    )
    return call(
        finish_kernel,
        None,
        [
            pltpu.VMEM((256, 128), F32),
            pltpu.VMEM((128, 256), F32),
            pltpu.VMEM(fields.shape, F32),
            pltpu.SemaphoreType.DMA((4,)),
        ],
        info, near(own), near(partner(away)), near(parity),
        result=jax.ShapeDtypeStruct(fields.shape, F32),
    )


def solution(mesh):
    in_specs = (P(None, "net", "wide", "narrow"), P(), P(), P())
    out_specs = P(None, "net", "wide", "narrow")
    return jax.shard_map(
        per_device, mesh=mesh, in_specs=in_specs, out_specs=out_specs, check_vma=False
    )
```
